256 devices in a mesh: gx: 16 (over z, core), gy: 8 (over x, y_hi), gz: 2 (over y_lo).
Axes of the slice: x: 4, y: 4 (y_hi: 2, y_lo: 2; y = y_hi * 2 + y_lo), z: 8, core: 2. Of those that a mesh axis runs over, the one named last changes fastest.
Arguments:
- body_force: bfloat16 [3, 256, 512, 256], P(None, 'gx', ('gy', 'gz')), may hold values from -6 to 6
- solid_mask: int32 [256, 512, 256], P('gx', ('gy', 'gz')), may hold values 0 or 1
- tracers: float32 [2, 256, 512, 256], P(None, 'gx', 'gy', 'gz'), may hold values from 0 to 1
- inlet_mask: int32 [2, 512, 256], P(None, 'gy', 'gz'), may hold values 0 or 1
Outputs:
- velocity: float32 [3, 256, 512, 256], P(None, 'gx', 'gy', 'gz')
- concentration: float32 [2, 256, 512, 256], P(None, 'gx', 'gy', 'gz')
The draws below stay inside these ranges and needn't reach their ends.
All inputs are finite; a program needn't handle non-finite values. No bound on the sum of `solid_mask` or of `inlet_mask` on one device may be relied on, other than what follows from the above.
Results may differ from the reference program's by a relative error of at most 0.012.
Values may be sent and summed in bfloat16 or wider, within the bound.
A program may use at most 128 MiB of HBM per device.

```python
import math
import jax
import jax.numpy as jnp
from jax import lax

STEPS = 4
GRID_X = 256
GRID_Y = 512
GRID_Z = 256


def with_ends(drawn, own_key, least, largest):
    index_at = [jax.random.randint(jax.random.fold_in(own_key, axis), (), 0, length) for axis, length in enumerate(drawn.shape)]
    main_axis = drawn.shape.index(max(drawn.shape))
    next_to = index_at[:main_axis] + [(index_at[main_axis] + 1) % drawn.shape[main_axis]] + index_at[main_axis + 1:]
    return drawn.at[tuple(index_at)].set(least).at[tuple(next_to)].set(largest)


def steps_of(stream_key, shape, cuts, least, top_value):
    def one(position, parts):
        heights = jax.random.uniform(jax.random.fold_in(jax.random.fold_in(stream_key, 6), position), (parts,), jnp.float32, least / len(cuts), top_value / len(cuts))
        return jnp.repeat(jnp.exp(heights), shape[position] // parts).reshape((-1,) + (1,) * (len(shape) - position - 1))

    level = one(*cuts[0])
    for cut in cuts[1:]:
        level = level * one(*cut)
    return level


def noise(own_key, extent, spread, bound, shards=(), kind=jnp.bfloat16):
    level = steps_of(own_key, extent, shards, -0.22, 0.18) if shards else 1.0
    values = jax.random.normal(own_key, extent, jnp.float32) * spread * level
    return jnp.minimum(jnp.maximum(values, -bound), bound).astype(kind)


def setup_inputs(seed: int = 0) -> dict:
    seeds = jax.random.split(jax.random.key(seed), 5)
    return {
        "body_force": noise(seeds[0], (3, GRID_X, GRID_Y, GRID_Z), 1.0, 6.0, ((1, 16), (2, 16))),
        "solid_mask": with_ends((jax.random.randint(seeds[1], (GRID_X, GRID_Y, GRID_Z), 0, 5) < 2).astype(jnp.int32), jax.random.fold_in(seeds[1], 1), 0, 1),
        "tracers": jnp.clip(1.0 * jax.random.uniform(seeds[2], (2, GRID_X, GRID_Y, GRID_Z), jnp.float32) ** steps_of(seeds[2], (2, GRID_X, GRID_Y, GRID_Z), ((1, 16), (2, 8), (3, 2)), -0.2, 0.2), 0.0, 1.0),
        "inlet_mask": with_ends((jax.random.randint(seeds[3], (2, GRID_Y, GRID_Z), 0, 2) < 1).astype(jnp.int32), jax.random.fold_in(seeds[3], 1), 0, 1),
    }


viscosity = 0.0625
screening = 0.25
time_step = 0.1


def tables(length):
    index = jnp.arange(length).astype(jnp.int32)
    phase = ((index[:, None] * index[None, :]) % length).astype(jnp.float32) * (2.0 * math.pi / length)
    return jnp.cos(phase).astype(jnp.bfloat16), jnp.sin(phase).astype(jnp.bfloat16)


def wavenumber(index, length):
    signed = jnp.where(index < length // 2, index, index - length)
    signed = jnp.where(index == length // 2, 0, signed)
    return signed.astype(jnp.float32) * (2.0 * math.pi / length)


def ein(form, table, data):
    return jnp.einsum(form, table.astype(jnp.float32), data.astype(jnp.float32), precision=lax.Precision.HIGHEST)


def project(spectrum, waves, wave_sq, gain):
    inner = waves[0] * spectrum[0] + waves[1] * spectrum[1] + waves[2] * spectrum[2]
    along = jnp.where(wave_sq > 0, inner / jnp.where(wave_sq > 0, wave_sq, 1.0), 0.0)
    return jnp.stack([gain * (spectrum[0] - waves[0] * along), gain * (spectrum[1] - waves[1] * along), gain * (spectrum[2] - waves[2] * along)])


def reference(body_force, solid_mask, tracers, inlet_mask):
    forcing = body_force * (1 - solid_mask).astype(jnp.bfloat16)[None]
    cos_z, sin_z = tables(GRID_Z)
    cos_y, sin_y = tables(GRID_Y)
    cos_x, sin_x = tables(GRID_X)
    real_z = ein("kn,ixyn->ixyk", cos_z, forcing).astype(jnp.bfloat16)
    imag_z = (-ein("kn,ixyn->ixyk", sin_z, forcing)).astype(jnp.bfloat16)
    real_y = (ein("kn,ixnz->ixkz", cos_y, real_z) + ein("kn,ixnz->ixkz", sin_y, imag_z)).astype(jnp.bfloat16)
    imag_y = (ein("kn,ixnz->ixkz", cos_y, imag_z) - ein("kn,ixnz->ixkz", sin_y, real_z)).astype(jnp.bfloat16)
    real_x = ein("kn,inyz->ikyz", cos_x, real_y) + ein("kn,inyz->ikyz", sin_x, imag_y)
    imag_x = ein("kn,inyz->ikyz", cos_x, imag_y) - ein("kn,inyz->ikyz", sin_x, real_y)
    wave_x = wavenumber(jnp.arange(GRID_X).astype(jnp.int32), GRID_X)[:, None, None]
    wave_y = wavenumber(jnp.arange(GRID_Y).astype(jnp.int32), GRID_Y)[None, :, None]
    wave_z = wavenumber(jnp.arange(GRID_Z).astype(jnp.int32), GRID_Z)[None, None, :]
    wave_sq = wave_x * wave_x + wave_y * wave_y + wave_z * wave_z
    gain = 1.0 / ((viscosity * wave_sq + screening) * float(GRID_X * GRID_Y * GRID_Z))
    waves = (wave_x, wave_y, wave_z)
    green_real = project(real_x, waves, wave_sq, gain).astype(jnp.bfloat16)
    green_imag = project(imag_x, waves, wave_sq, gain).astype(jnp.bfloat16)
    back_real = (ein("kn,ikyz->inyz", cos_x, green_real) - ein("kn,ikyz->inyz", sin_x, green_imag)).astype(jnp.bfloat16)
    back_imag = (ein("kn,ikyz->inyz", sin_x, green_real) + ein("kn,ikyz->inyz", cos_x, green_imag)).astype(jnp.bfloat16)
    rows_real = (ein("kn,ixkz->ixnz", cos_y, back_real) - ein("kn,ixkz->ixnz", sin_y, back_imag)).astype(jnp.bfloat16)
    rows_imag = (ein("kn,ixkz->ixnz", sin_y, back_real) + ein("kn,ixkz->ixnz", cos_y, back_imag)).astype(jnp.bfloat16)
    velocity = ein("kn,ixyk->ixyn", cos_z, rows_real) - ein("kn,ixyk->ixyn", sin_z, rows_imag)
    first_plane = (jnp.arange(GRID_X).astype(jnp.int32) == 0)[None, :, None, None]
    inlet = first_plane & (inlet_mask == 1)[:, None, :, :]
    conc = jnp.where(inlet, jnp.float32(1.0), tracers)
    rates = jnp.array([0.05, 0.15], dtype=jnp.float32)[:, None, None, None]
    for step_index in range(STEPS):
        transport = jnp.zeros_like(conc)
        laplace = jnp.zeros_like(conc)
        for dim in (1, 2, 3):
            lower = jnp.roll(conc, 1, axis=dim)
            lower_two = jnp.roll(conc, 2, axis=dim)
            upper = jnp.roll(conc, -1, axis=dim)
            upper_two = jnp.roll(conc, -2, axis=dim)
            speed = velocity[dim - 1][None]
            behind = 1.5 * conc - 2.0 * lower + 0.5 * lower_two
            ahead = -1.5 * conc + 2.0 * upper - 0.5 * upper_two
            transport = transport + jnp.maximum(speed, 0.0) * behind + jnp.minimum(speed, 0.0) * ahead
            laplace = laplace + upper + lower - 2.0 * conc
        conc = conc - time_step * transport + time_step * rates * laplace
    return velocity, conc
```

```python
import functools
import math

import jax
import jax.numpy as jnp
import numpy as np
from jax import lax
from jax.experimental import pallas as pl
from jax.experimental.pallas import tpu as pltpu
from jax.sharding import PartitionSpec as P

STEPS = 4
VISCOSITY = 0.0625
SCREENING = 0.25
TIME_STEP = 0.1
RATES = (0.05, 0.15)

MESH = pl.DeviceIdType.MESH
BF16 = jnp.bfloat16
F32 = jnp.float32
GRID_X, GRID_Y, GRID_Z = 256, 512, 256
KZ = GRID_Z // 2
VMEM_LIMIT = 60 * 1024 * 1024


def cos_sin(length):
    index = np.arange(length)
    phase = (index[:, None] * index[None, :] % length) * (2.0 * math.pi / length)
    return np.cos(phase), np.sin(phase)


def z_tables():
    cos_t, sin_t = cos_sin(GRID_Z)
    forward = np.concatenate([cos_t[:, :KZ], -sin_t[:, :KZ]], axis=1)
    forward[:, KZ] = cos_t[:, KZ]
    inverse = np.concatenate([2.0 * cos_t[:KZ], -2.0 * sin_t[:KZ]], axis=0)
    inverse[0] = cos_t[0]
    inverse[KZ] = cos_t[KZ]
    return forward.astype(jnp.bfloat16), inverse.astype(jnp.bfloat16)


def y_table():
    cos_t, sin_t = cos_sin(GRID_Y)
    return np.concatenate([cos_t, sin_t], axis=1).astype(jnp.bfloat16)


def x_tables():
    cos_t, sin_t = cos_sin(GRID_X)
    order = np.arange(GRID_X).reshape(2, 8, 16).transpose(0, 2, 1).reshape(-1)
    cos_p, sin_p = cos_t[order], sin_t[order]
    forward = np.block([[cos_p, -sin_p], [sin_p, cos_p]])
    inverse = np.block([[cos_p.T, sin_p.T], [-sin_p.T, cos_p.T]])
    return forward.astype(jnp.bfloat16), inverse.astype(jnp.bfloat16)


def swap_index_and_lanes(parts, unit):
    lane = lax.broadcasted_iota(jnp.int32, parts[0].shape, 1)
    step = 1
    while step < len(parts):
        shift = unit * step
        upper = (lane & shift) != 0
        after = list(parts)
        for a in range(len(parts)):
            if a & step:
                continue
            low, high = parts[a], parts[a | step]
            after[a] = jnp.where(upper, pltpu.roll(high, shift, 1), low)
            after[a | step] = jnp.where(upper, high, pltpu.roll(low, 128 - shift, 1))
        parts = after
        step *= 2
    return parts


def signed_wave(index, length):
    signed = jnp.where(index < length // 2, index, index - length)
    signed = jnp.where(index == length // 2, 0, signed)
    return signed.astype(F32) * (2.0 * math.pi / length)


def spectral_kernel(
    force_hbm, mask_hbm, fz_hbm, iz_hbm, ty_hbm, fx_hbm, ix_hbm, vel_ref,
    force, mask, fz, iz, ty, fx, ix, zbuf, rhs, xin, spec, green, zin,
    send1, recv1, send2, recv2, send3, recv3, send4, recv4, sendv, recvv,
    load_sem, send_sem, recv_sem, vsend_sem, vrecv_sem,
):
    gx, gy, gz = lax.axis_index("gx"), lax.axis_index("gy"), lax.axis_index("gz")
    group = gy * 2 + gz

    def in_plane(to):
        return (gx, to // 2, to % 2)

    def in_column(to):
        return (to, gy, gz)

    loads = [
        pltpu.make_async_copy(src, dst, load_sem.at[n])
        for n, (src, dst) in enumerate(
            [(fz_hbm, fz), (mask_hbm, mask), (force_hbm, force), (ty_hbm, ty), (fx_hbm, fx), (ix_hbm, ix), (iz_hbm, iz)]
        )
    ]
    for load in loads:
        load.start()

    barrier = pltpu.get_barrier_semaphore()

    def greet(k, carry):
        pl.semaphore_signal(barrier, inc=1, device_id=in_plane((group + k) % 16), device_id_type=MESH)
        pl.semaphore_signal(barrier, inc=1, device_id=in_column((gx + k) % 16), device_id_type=MESH)
        return carry

    lax.fori_loop(1, 16, greet, 0)

    def exchange(stage, c, send, recv, me, place):
        def one(k, carry):
            to = (me + k) % 16
            pltpu.make_async_remote_copy(
                src_ref=send.at[c, to], dst_ref=recv.at[c, me],
                send_sem=send_sem.at[stage, c], recv_sem=recv_sem.at[stage, c],
                device_id=place(to), device_id_type=MESH,
            ).start()
            return carry

        lax.fori_loop(1, 16, one, 0)
        pltpu.make_async_copy(send.at[c, me], recv.at[c, me], recv_sem.at[stage, c]).start()

    def arrived(stage, c, recv):
        pltpu.make_async_copy(recv.at[c], recv.at[c], recv_sem.at[stage, c]).wait()

    def sent(stage, c, send):
        pltpu.make_async_copy(send.at[c, pl.ds(0, 15)], send.at[c, pl.ds(0, 15)], send_sem.at[stage, c]).wait()

    for load in loads[:3]:
        load.wait()

    def forward_z(c, carry):
        for h in range(2):
            rows = slice(8 * h, 8 * h + 8)
            kept = jnp.where(mask[rows] == 0, force[c, rows].astype(F32), 0.0).astype(BF16)
            out = jnp.dot(kept.reshape(256, 256), fz[...], preferred_element_type=F32)
            zbuf[rows] = out.reshape(8, 32, 256)
        for ri in range(2):
            for y in (0, 16):
                parts = [zbuf[x, y:y + 16, 128 * ri:128 * ri + 128] for x in range(16)]
                parts = swap_index_and_lanes(parts, 8)
                for to in range(16):
                    send1[c, to, ri, y:y + 16, :] = parts[to].astype(BF16)

        @pl.when(c == 0)
        def _():
            pl.semaphore_wait(barrier, 30)

        exchange(0, c, send1, recv1, group, in_plane)
        return carry

    lax.fori_loop(0, 3, forward_z, 0)

    def y_transform(recv, send, c, forward):
        re = recv[c, :, 0].reshape(512, 128)
        im = recv[c, :, 1].reshape(512, 128)
        rhs[0:512, 0:128] = re
        rhs[0:512, 128:256] = im
        rhs[512:1024, 0:128] = im if forward else -im
        rhs[512:1024, 128:256] = -re if forward else re
        for h in range(2):
            out = jnp.dot(ty[256 * h:256 * h + 256, :], rhs[...], preferred_element_type=F32)
            out = out.astype(BF16).reshape(8, 32, 256)
            send[c, 8 * h:8 * h + 8, 0] = out[:, :, 0:128]
            send[c, 8 * h:8 * h + 8, 1] = out[:, :, 128:256]

    loads[3].wait()

    def forward_y(c, carry):
        arrived(0, c, recv1)
        y_transform(recv1, send2, c, True)
        exchange(1, c, send2, recv2, gx, in_column)
        return carry

    lax.fori_loop(0, 3, forward_y, 0)

    loads[4].wait()

    def forward_x(c, carry):
        arrived(1, c, recv2)
        for ri in range(2):
            for hi in range(2):
                for ky in (0, 16):
                    parts = [recv2[c, 8 * hi + i, ri, ky:ky + 16, :].astype(F32) for i in range(8)]
                    parts = swap_index_and_lanes(parts, 1)
                    lanes = slice(256 * ri + 128 * hi, 256 * ri + 128 * hi + 128)
                    for k in range(8):
                        xin[k, ky:ky + 16, lanes] = parts[k].astype(BF16)
        spec[c] = jnp.dot(xin[...].reshape(256, 512), fx[...], preferred_element_type=F32)
        return carry

    lax.fori_loop(0, 3, forward_x, 0)

    wave_x = signed_wave(lax.broadcasted_iota(jnp.int32, (16, GRID_X), 1), GRID_X)
    row = lax.broadcasted_iota(jnp.int32, (16, GRID_X), 0)

    def project(b, carry):
        at = pl.ds(pl.multiple_of(b * 16, 16), 16)
        wave_y = signed_wave(gx * 32 + (b % 2) * 16 + row, GRID_Y)
        wave_z = signed_wave(group * 8 + b // 2 + jnp.zeros_like(row), GRID_Z)
        wave_sq = wave_x * wave_x + wave_y * wave_y + wave_z * wave_z
        gain = 1.0 / ((VISCOSITY * wave_sq + SCREENING) * float(GRID_X * GRID_Y * GRID_Z))
        inverse_sq = jnp.where(wave_sq > 0, 1.0 / jnp.where(wave_sq > 0, wave_sq, 1.0), 0.0)
        waves = (wave_x, wave_y, wave_z)
        for lanes in (slice(0, 256), slice(256, 512)):
            parts = [spec[c, at, lanes] for c in range(3)]
            inner = waves[0] * parts[0] + waves[1] * parts[1] + waves[2] * parts[2]
            along = inner * inverse_sq
            for c in range(3):
                green[c, at, lanes] = (gain * (parts[c] - waves[c] * along)).astype(BF16)
        return carry

    lax.fori_loop(0, 16, project, 0)

    loads[5].wait()

    def inverse_x(c, carry):
        spec[c] = jnp.dot(green[c], ix[...], preferred_element_type=F32)
        for ro in range(2):
            for hi in range(2):
                for ky in (0, 16):
                    first = 256 * ro + 128 * hi
                    parts = [spec[c, 32 * k + ky:32 * k + ky + 16, first:first + 128] for k in range(8)]
                    parts = swap_index_and_lanes(parts, 1)
                    for i in range(8):
                        send3[c, 8 * hi + i, ro, ky:ky + 16, :] = parts[i].astype(BF16)
        exchange(2, c, send3, recv3, gx, in_column)
        return carry

    lax.fori_loop(0, 3, inverse_x, 0)

    def inverse_y(c, carry):
        arrived(2, c, recv3)
        y_transform(recv3, send4, c, False)
        exchange(3, c, send4, recv4, group, in_plane)
        return carry

    lax.fori_loop(0, 3, inverse_y, 0)

    loads[6].wait()
    own = pl.multiple_of(gz * 32, 32)
    other = pl.multiple_of((1 - gz) * 32, 32)

    def to_partner(c):
        return pltpu.make_async_remote_copy(
            src_ref=sendv.at[c], dst_ref=recvv.at[c], send_sem=vsend_sem.at[c], recv_sem=vrecv_sem.at[c],
            device_id=(gx, gy, 1 - gz), device_id_type=MESH,
        )

    def inverse_z(c, carry):
        arrived(3, c, recv4)
        for ro in range(2):
            for y in (0, 16):
                parts = [recv4[c, s, ro, y:y + 16, :].astype(F32) for s in range(16)]
                parts = swap_index_and_lanes(parts, 8)
                for x in range(16):
                    zin[x, y:y + 16, 128 * ro:128 * ro + 128] = parts[x].astype(BF16)
        for h in range(2):
            rows = slice(8 * h, 8 * h + 8)
            out = jnp.dot(zin[rows].reshape(256, 256), iz[...], preferred_element_type=F32)
            zbuf[rows] = out.reshape(8, 32, 256)
        mine = pl.ds(pl.multiple_of(gz * 128, 128), 128)
        theirs = pl.ds(pl.multiple_of((1 - gz) * 128, 128), 128)
        sendv[c] = zbuf[:, :, theirs].astype(BF16)
        to_partner(c).start()
        vel_ref[c, :, pl.ds(own, 32), :] = zbuf[:, :, mine]
        return carry

    lax.fori_loop(0, 3, inverse_z, 0)

    def gather(c, carry):
        to_partner(c).wait_recv()
        vel_ref[c, :, pl.ds(other, 32), :] = recvv[c].astype(F32)
        return carry

    lax.fori_loop(0, 3, gather, 0)

    def finish(c, carry):
        sent(0, c, send1)
        sent(1, c, send2)
        sent(2, c, send3)
        sent(3, c, send4)
        to_partner(c).wait_send()
        return carry

    lax.fori_loop(0, 3, finish, 0)


def spectral(body_force, solid_mask):
    fz, iz = z_tables()
    fx, ix = x_tables()
    ty = y_table()
    any_spec = pl.BlockSpec(memory_space=pl.ANY)
    slab = (3, 16, 2, 32, 128)
    dma = pltpu.SemaphoreType.DMA
    return pl.pallas_call(
        spectral_kernel,
        out_shape=jax.ShapeDtypeStruct((3, 16, 64, 128), F32),
        in_specs=[any_spec] * 7,
        out_specs=pl.BlockSpec(memory_space=pltpu.VMEM),
        scratch_shapes=[
            pltpu.VMEM((3, 16, 32, 256), BF16),
            pltpu.VMEM((16, 32, 256), jnp.int32),
            pltpu.VMEM((256, 256), BF16),
            pltpu.VMEM((256, 256), BF16),
            pltpu.VMEM((512, 1024), BF16),
            pltpu.VMEM((512, 512), BF16),
            pltpu.VMEM((512, 512), BF16),
            pltpu.VMEM((16, 32, 256), F32),
            pltpu.VMEM((1024, 256), BF16),
            pltpu.VMEM((8, 32, 512), BF16),
            pltpu.VMEM((3, 256, 512), F32),
            pltpu.VMEM((3, 256, 512), BF16),
            pltpu.VMEM((16, 32, 256), BF16),
        ]
        + [pltpu.VMEM(slab, BF16)] * 8
        + [pltpu.VMEM((3, 16, 32, 128), BF16)] * 2
        + [dma((7,)), dma((4, 3)), dma((4, 3)), dma((3,)), dma((3,))],
        compiler_params=pltpu.CompilerParams(
            collective_id=0, has_side_effects=True, vmem_limit_bytes=VMEM_LIMIT
        ),
        cost_estimate=pl.CostEstimate(flops=4_000_000_000, bytes_accessed=8_000_000, transcendentals=0),
        name="spectral",
    )(body_force, solid_mask, jnp.asarray(fz), jnp.asarray(iz), jnp.asarray(ty), jnp.asarray(fx), jnp.asarray(ix))


def transport_kernel(
    vel, tracers, inlet, out_ref, state, ysend, yrecv, zsend, zrecv,
    xs_sem, xr_sem, ys_sem, yr_sem, zs_sem, zr_sem,
):
    gx, gy, gz = lax.axis_index("gx"), lax.axis_index("gy"), lax.axis_index("gz")
    x_next, x_last = (gx + 1) % 16, (gx + 15) % 16
    y_next, y_last = (gy + 1) % 8, (gy + 7) % 8
    neighbours = ((x_next, gy, gz), (x_last, gy, gz), (gx, y_next, gz), (gx, y_last, gz), (gx, gy, 1 - gz))

    barrier = pltpu.get_barrier_semaphore()
    for place in neighbours:
        pl.semaphore_signal(barrier, inc=1, device_id=place, device_id_type=MESH)

    for t in range(2):
        state[0, t, 2:18, 8:72, :] = tracers[t]
        injected = jnp.where(inlet[t] == 1, 1.0, tracers[t, 0])
        state[0, t, 2, 8:72, :] = jnp.where(gx == 0, injected, tracers[t, 0])

    pl.semaphore_wait(barrier, 5)
    lane = lax.broadcasted_iota(jnp.int32, (64, 128), 1)

    def copies(step):
        def remote(src, dst, send, recv, place):
            return pltpu.make_async_remote_copy(
                src_ref=src, dst_ref=dst, send_sem=send, recv_sem=recv, device_id=place, device_id_type=MESH
            )

        return (
            remote(state.at[step, :, pl.ds(16, 2), pl.ds(8, 64)], state.at[step, :, pl.ds(0, 2), pl.ds(8, 64)],
                   xs_sem.at[step, 0], xr_sem.at[step, 0], neighbours[0]),
            remote(state.at[step, :, pl.ds(2, 2), pl.ds(8, 64)], state.at[step, :, pl.ds(18, 2), pl.ds(8, 64)],
                   xs_sem.at[step, 1], xr_sem.at[step, 1], neighbours[1]),
            remote(ysend.at[step, 0], yrecv.at[step, 0], ys_sem.at[step, 0], yr_sem.at[step, 0], neighbours[2]),
            remote(ysend.at[step, 1], yrecv.at[step, 1], ys_sem.at[step, 1], yr_sem.at[step, 1], neighbours[3]),
            remote(zsend.at[step], zrecv.at[step], zs_sem.at[step], zr_sem.at[step], neighbours[4]),
        )

    def advance(step, last):
        sends = copies(step)
        sends[0].start()
        sends[1].start()
        for t in range(2):
            for x in range(16):
                row = slice(2 * (x % 4), 2 * (x % 4) + 2)
                ysend[step, 0, t, x // 4, row, :] = state[step, t, 2 + x, 70:72, :]
                ysend[step, 1, t, x // 4, row, :] = state[step, t, 2 + x, 8:10, :]
        sends[2].start()
        sends[3].start()
        packed = jnp.zeros((64, 128), F32)
        for s in range(32):
            edge = pltpu.roll(state[step, s // 16, 2 + s % 16, 8:72, :], (2 + 4 * s) % 128, 1)
            packed = jnp.where(lane // 4 == s, edge, packed)
        zsend[step] = packed
        sends[4].start()
        for send in sends:
            send.wait_recv()
        for t in range(2):
            for x in range(16):
                row = slice(2 * (x % 4), 2 * (x % 4) + 2)
                state[step, t, 2 + x, 6:8, :] = yrecv[step, 0, t, x // 4, row, :]
                state[step, t, 2 + x, 72:74, :] = yrecv[step, 1, t, x // 4, row, :]

        narrow = lax.broadcasted_iota(jnp.int32, (16, 128), 1)

        def plane(x, carry):
            for y in range(0, 64, 16):
                speeds = [vel[d, x, y:y + 16, :] * (-TIME_STEP) for d in range(3)]
                toward = [jnp.minimum(s, 0.0) for s in speeds]
                away = [jnp.maximum(s, 0.0) for s in speeds]
                for t in range(2):
                    rate = TIME_STEP * RATES[t]
                    conc = state[step, t, 2 + x, 8 + y:24 + y, :]

                    def shifted_x(k):
                        return state[step, t, 2 + x + k, 8 + y:24 + y, :]

                    def shifted_y(k):
                        return state[step, t, 2 + x, 8 + y + k:24 + y + k, :]

                    ends = zrecv[step, y:y + 16, :]
                    slot = 4 * (16 * t + x)
                    ends = pltpu.roll(ends, (254 - slot) % 128, 1)
                    wrapped = {-1: narrow == 127, -2: narrow >= 126, 1: narrow == 0, 2: narrow < 2}

                    def shifted_z(k):
                        return pltpu.roll(jnp.where(wrapped[k], ends, conc), -k % 128, 1)

                    total = conc
                    for d, shifted in enumerate((shifted_x, shifted_y, shifted_z)):
                        low, low_two, high, high_two = shifted(-1), shifted(-2), shifted(1), shifted(2)
                        total = total + (1.5 * toward[d] - rate) * (conc - low)
                        total = total - (0.5 * toward[d]) * (low - low_two)
                        total = total + (1.5 * away[d] + rate) * (high - conc)
                        total = total - (0.5 * away[d]) * (high_two - high)
                    if last:
                        out_ref[t, x, y:y + 16, :] = total
                    else:
                        state[step + 1, t, 2 + x, 8 + y:24 + y, :] = total
            return carry

        lax.fori_loop(0, 16, plane, 0)

    def run(step, carry):
        advance(step, False)
        return carry

    lax.fori_loop(0, STEPS - 1, run, 0)
    advance(STEPS - 1, True)

    def finish(step, carry):
        for send in copies(step):
            send.wait_send()
        return carry

    lax.fori_loop(0, STEPS, finish, 0)


def transport(velocity, tracers, inlet_mask):
    vmem = pl.BlockSpec(memory_space=pltpu.VMEM)
    dma = pltpu.SemaphoreType.DMA
    return pl.pallas_call(
        transport_kernel,
        out_shape=jax.ShapeDtypeStruct((2, 16, 64, 128), F32),
        in_specs=[vmem] * 3,
        out_specs=vmem,
        scratch_shapes=[
            pltpu.VMEM((STEPS, 2, 20, 80, 128), F32),
            pltpu.VMEM((STEPS, 2, 2, 4, 8, 128), F32),
            pltpu.VMEM((STEPS, 2, 2, 4, 8, 128), F32),
            pltpu.VMEM((STEPS, 64, 128), F32),
            pltpu.VMEM((STEPS, 64, 128), F32),
            dma((STEPS, 2)), dma((STEPS, 2)), dma((STEPS, 2)), dma((STEPS, 2)), dma((STEPS,)), dma((STEPS,)),
        ],
        compiler_params=pltpu.CompilerParams(
            collective_id=1, has_side_effects=True, vmem_limit_bytes=VMEM_LIMIT
        ),
        cost_estimate=pl.CostEstimate(flops=60_000_000, bytes_accessed=5_000_000, transcendentals=0),
        name="transport",
    )(velocity, tracers, inlet_mask)


def per_device(body_force, solid_mask, tracers, inlet_mask):
    velocity = spectral(body_force, solid_mask)
    return velocity, transport(velocity, tracers, inlet_mask)


def solution(mesh):
    in_specs = (
        P(None, "gx", ("gy", "gz"), None),
        P("gx", ("gy", "gz"), None),
        P(None, "gx", "gy", "gz"),
        P(None, "gy", "gz"),
    )
    out_specs = (P(None, "gx", "gy", "gz"), P(None, "gx", "gy", "gz"))
    return jax.shard_map(per_device, mesh=mesh, in_specs=in_specs, out_specs=out_specs, check_vma=False)
```

```python
import math

import jax
import jax.numpy as jnp
import numpy as np
from jax import lax
from jax.experimental import pallas as pl
from jax.experimental.pallas import tpu as pltpu
from jax.sharding import PartitionSpec as P

STEPS = 4
VISCOSITY = 0.0625
SCREENING = 0.25
TIME_STEP = 0.1
RATES = (0.05, 0.15)

MESH = pl.DeviceIdType.MESH
BF16 = jnp.bfloat16
F32 = jnp.float32
GRID_X, GRID_Y, GRID_Z = 256, 512, 256
KZ = GRID_Z // 2
VMEM_LIMIT = 60 * 1024 * 1024


def cos_sin(length):
    index = np.arange(length)
    phase = (index[:, None] * index[None, :] % length) * (2.0 * math.pi / length)
    return np.cos(phase), np.sin(phase)


def z_tables():
    cos_t, sin_t = cos_sin(GRID_Z)
    forward = np.concatenate([cos_t[:, :KZ], -sin_t[:, :KZ]], axis=1)
    forward[:, KZ] = cos_t[:, KZ]
    inverse = np.concatenate([2.0 * cos_t[:KZ], -2.0 * sin_t[:KZ]], axis=0)
    inverse[0] = cos_t[0]
    inverse[KZ] = cos_t[KZ]
    return forward.astype(jnp.bfloat16), inverse.astype(jnp.bfloat16)


def y_table():
    cos_t, sin_t = cos_sin(GRID_Y)
    return np.concatenate([cos_t, sin_t], axis=1).astype(jnp.bfloat16)


def x_tables():
    cos_t, sin_t = cos_sin(GRID_X)
    order = np.arange(GRID_X).reshape(2, 8, 16).transpose(0, 2, 1).reshape(-1)
    cos_p, sin_p = cos_t[order], sin_t[order]
    forward = np.block([[cos_p, -sin_p], [sin_p, cos_p]])
    inverse = np.block([[cos_p.T, sin_p.T], [-sin_p.T, cos_p.T]])
    return forward.astype(jnp.bfloat16), inverse.astype(jnp.bfloat16)


def swap_index_and_lanes(parts, unit):
    lane = lax.broadcasted_iota(jnp.int32, parts[0].shape, 1)
    step = 1
    while step < len(parts):
        shift = unit * step
        upper = (lane & shift) != 0
        after = list(parts)
        for a in range(len(parts)):
            if a & step:
                continue
            low, high = parts[a], parts[a | step]
            after[a] = jnp.where(upper, pltpu.roll(high, shift, 1), low)
            after[a | step] = jnp.where(upper, high, pltpu.roll(low, 128 - shift, 1))
        parts = after
        step *= 2
    return parts


def signed_wave(index, length):
    signed = jnp.where(index < length // 2, index, index - length)
    signed = jnp.where(index == length // 2, 0, signed)
    return signed.astype(F32) * (2.0 * math.pi / length)


TILES = ((0, 1, 14, 15), (2, 3, 4, 5), (6, 7, 8, 9), (10, 11, 12, 13))
GROUPS = ((0, 1), (1, 1), (2, 2))


def fused_kernel(
    force_hbm, mask_hbm, tracers_hbm, inlet_hbm, fz_hbm, iz_hbm, ty_hbm, fx_hbm, ix_hbm, vel_ref, out_ref,
    force, mask, fz, iz, ty, fx, ix, zbuf, rhs, xin, spec, green, zin,
    send1, recv1, send2, recv2, send3, recv3, send4, recv4, sendv, recvv,
    inlet, state, ends, stage, xsend, xrecv, ysend, yrecv, zsend, zrecv,
    load_sem, send_sem, recv_sem, vsend_sem, vrecv_sem, xs_sem, xr_sem, fs_sem, fr_sem,
):
    gx, gy, gz = lax.axis_index("gx"), lax.axis_index("gy"), lax.axis_index("gz")
    group = gy * 2 + gz

    def in_plane(to):
        return (gx, to // 2, to % 2)

    def in_column(to):
        return (to, gy, gz)

    loads = [
        pltpu.make_async_copy(src, dst, load_sem.at[n])
        for n, (src, dst) in enumerate(
            [(fz_hbm, fz), (mask_hbm, mask), (force_hbm, force), (ty_hbm, ty), (fx_hbm, fx), (ix_hbm, ix), (iz_hbm, iz),
             (inlet_hbm, inlet), (tracers_hbm, state.at[0, :, pl.ds(2, 16), pl.ds(8, 64)])]
        )
    ]
    for load in loads:
        load.start()

    barrier = pltpu.get_barrier_semaphore()

    def greet(k, carry):
        pl.semaphore_signal(barrier, inc=1, device_id=in_plane((group + k) % 16), device_id_type=MESH)
        pl.semaphore_signal(barrier, inc=1, device_id=in_column((gx + k) % 16), device_id_type=MESH)
        return carry

    lax.fori_loop(1, 16, greet, 0)

    def exchange(stage, c, send, recv, me, place):
        def one(k, carry):
            to = (me + k) % 16
            pltpu.make_async_remote_copy(
                src_ref=send.at[c, to], dst_ref=recv.at[c, me],
                send_sem=send_sem.at[stage, c], recv_sem=recv_sem.at[stage, c],
                device_id=place(to), device_id_type=MESH,
            ).start()
            return carry

        lax.fori_loop(1, 16, one, 0)
        pltpu.make_async_copy(send.at[c, me], recv.at[c, me], recv_sem.at[stage, c]).start()

    def arrived(stage, c, recv):
        pltpu.make_async_copy(recv.at[c], recv.at[c], recv_sem.at[stage, c]).wait()

    def sent(stage, c, send):
        pltpu.make_async_copy(send.at[c, pl.ds(0, 15)], send.at[c, pl.ds(0, 15)], send_sem.at[stage, c]).wait()

    for load in loads[:3]:
        load.wait()

    def forward_z(c, carry):
        for h in range(2):
            rows = slice(8 * h, 8 * h + 8)
            kept = jnp.where(mask[rows] == 0, force[c, rows].astype(F32), 0.0).astype(BF16)
            out = jnp.dot(kept.reshape(256, 256), fz[...], preferred_element_type=F32)
            zbuf[rows] = out.reshape(8, 32, 256)
        for ri in range(2):
            for y in (0, 16):
                parts = [zbuf[x, y:y + 16, 128 * ri:128 * ri + 128] for x in range(16)]
                parts = swap_index_and_lanes(parts, 8)
                for to in range(16):
                    send1[c, to, ri, y:y + 16, :] = parts[to].astype(BF16)

        @pl.when(c == 0)
        def _():
            pl.semaphore_wait(barrier, 30)

        exchange(0, c, send1, recv1, group, in_plane)
        return carry

    lax.fori_loop(0, 3, forward_z, 0)

    def y_transform(recv, send, c, forward):
        re = recv[c, :, 0].reshape(512, 128)
        im = recv[c, :, 1].reshape(512, 128)
        rhs[0:512, 0:128] = re
        rhs[0:512, 128:256] = im
        rhs[512:1024, 0:128] = im if forward else -im
        rhs[512:1024, 128:256] = -re if forward else re
        for h in range(2):
            out = jnp.dot(ty[256 * h:256 * h + 256, :], rhs[...], preferred_element_type=F32)
            out = out.astype(BF16).reshape(8, 32, 256)
            send[c, 8 * h:8 * h + 8, 0] = out[:, :, 0:128]
            send[c, 8 * h:8 * h + 8, 1] = out[:, :, 128:256]

    loads[3].wait()

    def forward_y(c, carry):
        arrived(0, c, recv1)
        y_transform(recv1, send2, c, True)
        exchange(1, c, send2, recv2, gx, in_column)
        return carry

    lax.fori_loop(0, 3, forward_y, 0)

    halo = Halo(state, ends, stage, xsend, xrecv, ysend, yrecv, zsend, zrecv, xs_sem, xr_sem, fs_sem, fr_sem)
    loads[7].wait()
    loads[8].wait()
    for t in range(2):
        plane = state[0, t, 2, 8:72, :]
        state[0, t, 2, 8:72, :] = jnp.where(gx == 0, jnp.where(inlet[t] == 1, 1.0, plane), plane)
    for group_id in range(3):
        halo.send(0, group_id)

    loads[4].wait()

    def forward_x(c, carry):
        arrived(1, c, recv2)
        for ri in range(2):
            for hi in range(2):
                for ky in (0, 16):
                    parts = [recv2[c, 8 * hi + i, ri, ky:ky + 16, :].astype(F32) for i in range(8)]
                    parts = swap_index_and_lanes(parts, 1)
                    lanes = slice(256 * ri + 128 * hi, 256 * ri + 128 * hi + 128)
                    for k in range(8):
                        xin[k, ky:ky + 16, lanes] = parts[k].astype(BF16)
        spec[c] = jnp.dot(xin[...].reshape(256, 512), fx[...], preferred_element_type=F32)
        return carry

    lax.fori_loop(0, 3, forward_x, 0)

    wave_x = signed_wave(lax.broadcasted_iota(jnp.int32, (16, GRID_X), 1), GRID_X)
    row = lax.broadcasted_iota(jnp.int32, (16, GRID_X), 0)

    def project(b, carry):
        at = pl.ds(pl.multiple_of(b * 16, 16), 16)
        wave_y = signed_wave(gx * 32 + (b % 2) * 16 + row, GRID_Y)
        wave_z = signed_wave(group * 8 + b // 2 + jnp.zeros_like(row), GRID_Z)
        wave_sq = wave_x * wave_x + wave_y * wave_y + wave_z * wave_z
        gain = 1.0 / ((VISCOSITY * wave_sq + SCREENING) * float(GRID_X * GRID_Y * GRID_Z))
        inverse_sq = jnp.where(wave_sq > 0, 1.0 / jnp.where(wave_sq > 0, wave_sq, 1.0), 0.0)
        waves = (wave_x, wave_y, wave_z)
        for lanes in (slice(0, 256), slice(256, 512)):
            parts = [spec[c, at, lanes] for c in range(3)]
            inner = waves[0] * parts[0] + waves[1] * parts[1] + waves[2] * parts[2]
            along = inner * inverse_sq
            for c in range(3):
                green[c, at, lanes] = (gain * (parts[c] - waves[c] * along)).astype(BF16)
        return carry

    lax.fori_loop(0, 16, project, 0)

    loads[5].wait()

    def inverse_x(c, carry):
        spec[c] = jnp.dot(green[c], ix[...], preferred_element_type=F32)
        for ro in range(2):
            for hi in range(2):
                for ky in (0, 16):
                    first = 256 * ro + 128 * hi
                    parts = [spec[c, 32 * k + ky:32 * k + ky + 16, first:first + 128] for k in range(8)]
                    parts = swap_index_and_lanes(parts, 1)
                    for i in range(8):
                        send3[c, 8 * hi + i, ro, ky:ky + 16, :] = parts[i].astype(BF16)
        exchange(2, c, send3, recv3, gx, in_column)
        return carry

    lax.fori_loop(0, 3, inverse_x, 0)

    def inverse_y(c, carry):
        arrived(2, c, recv3)
        y_transform(recv3, send4, c, False)
        exchange(3, c, send4, recv4, group, in_plane)
        return carry

    lax.fori_loop(0, 3, inverse_y, 0)

    loads[6].wait()
    own = pl.multiple_of(gz * 32, 32)
    other = pl.multiple_of((1 - gz) * 32, 32)

    def to_partner(c):
        return pltpu.make_async_remote_copy(
            src_ref=sendv.at[c], dst_ref=recvv.at[c], send_sem=vsend_sem.at[c], recv_sem=vrecv_sem.at[c],
            device_id=(gx, gy, 1 - gz), device_id_type=MESH,
        )

    def inverse_z(c, carry):
        arrived(3, c, recv4)
        for ro in range(2):
            for y in (0, 16):
                parts = [recv4[c, s, ro, y:y + 16, :].astype(F32) for s in range(16)]
                parts = swap_index_and_lanes(parts, 8)
                for x in range(16):
                    zin[x, y:y + 16, 128 * ro:128 * ro + 128] = parts[x].astype(BF16)
        for h in range(2):
            rows = slice(8 * h, 8 * h + 8)
            out = jnp.dot(zin[rows].reshape(256, 256), iz[...], preferred_element_type=F32)
            zbuf[rows] = out.reshape(8, 32, 256)
        mine = pl.ds(pl.multiple_of(gz * 128, 128), 128)
        theirs = pl.ds(pl.multiple_of((1 - gz) * 128, 128), 128)
        sendv[c] = zbuf[:, :, theirs].astype(BF16)
        to_partner(c).start()
        vel_ref[c, :, pl.ds(own, 32), :] = zbuf[:, :, mine]
        return carry

    lax.fori_loop(0, 3, inverse_z, 0)

    def gather(c, carry):
        to_partner(c).wait_recv()
        vel_ref[c, :, pl.ds(other, 32), :] = recvv[c].astype(F32)
        return carry

    lax.fori_loop(0, 3, gather, 0)

    transport(vel_ref, out_ref, halo)

    def finish(c, carry):
        sent(0, c, send1)
        sent(1, c, send2)
        sent(2, c, send3)
        sent(3, c, send4)
        to_partner(c).wait_send()
        return carry

    lax.fori_loop(0, 3, finish, 0)


class Halo:
    def __init__(self, state, ends, stage, xsend, xrecv, ysend, yrecv, zsend, zrecv, xs_sem, xr_sem, fs_sem, fr_sem):
        self.state, self.ends, self.stage = state, ends, stage
        self.xsend, self.xrecv, self.ysend, self.yrecv = xsend, xrecv, ysend, yrecv
        self.zsend, self.zrecv = zsend, zrecv
        self.xs_sem, self.xr_sem, self.fs_sem, self.fr_sem = xs_sem, xr_sem, fs_sem, fr_sem

    def copies(self, step, group_id):
        gx, gy, gz = lax.axis_index("gx"), lax.axis_index("gy"), lax.axis_index("gz")

        def remote(src, dst, send, recv, place):
            return pltpu.make_async_remote_copy(
                src_ref=src, dst_ref=dst, send_sem=send, recv_sem=recv, device_id=place, device_id_type=MESH
            )

        tiles = pl.ds(*GROUPS[group_id])
        found = [
            remote(self.ysend.at[step, side, tiles], self.yrecv.at[step, side, tiles],
                   self.fs_sem.at[step, group_id, side], self.fr_sem.at[step, group_id, side], place)
            for side, place in enumerate(((gx, (gy + 1) % 8, gz), (gx, (gy + 7) % 8, gz)))
        ]
        found.append(
            remote(self.zsend.at[step, tiles], self.zrecv.at[step, tiles],
                   self.fs_sem.at[step, group_id, 2], self.fr_sem.at[step, group_id, 2], (gx, gy, 1 - gz))
        )
        if group_id == 0:
            found += [
                remote(self.xsend.at[step, side], self.xrecv.at[step, side],
                       self.xs_sem.at[step, side], self.xr_sem.at[step, side], place)
                for side, place in enumerate((((gx + 1) % 16, gy, gz), ((gx + 15) % 16, gy, gz)))
            ]
        return found

    def send(self, step, group_id):
        state = self.state
        first, count = GROUPS[group_id]
        copies = self.copies(step, group_id)
        if group_id == 0:
            self.xsend[step, 0] = state[step, :, 16:18, 8:72, :].astype(BF16)
            self.xsend[step, 1] = state[step, :, 2:4, 8:72, :].astype(BF16)
            copies[3].start()
            copies[4].start()
        slot = lax.broadcasted_iota(jnp.int32, (16, 128), 1) // 4
        for tile in range(first, first + count):
            packed = jnp.zeros((16, 128), F32)
            for t in range(2):
                for i, x in enumerate(TILES[tile]):
                    slab = 4 * t + i
                    self.stage[0, 2 * slab:2 * slab + 2, :] = state[step, t, 2 + x, 70:72, :]
                    self.stage[1, 2 * slab:2 * slab + 2, :] = state[step, t, 2 + x, 8:10, :]
                    for b in range(4):
                        edge = pltpu.roll(
                            state[step, t, 2 + x, 8 + 16 * b:24 + 16 * b, :], (2 + 32 * b + 4 * slab) % 128, 1
                        )
                        packed = jnp.where(slot == 8 * b + slab, edge, packed)
            self.ysend[step, 0, tile] = self.stage[0].astype(BF16)
            self.ysend[step, 1, tile] = self.stage[1].astype(BF16)
            self.zsend[step, tile] = packed.astype(BF16)
        for copy in copies[:3]:
            copy.start()

    def receive(self, step, group_id):
        state = self.state
        first, count = GROUPS[group_id]
        for copy in self.copies(step, group_id):
            copy.wait_recv()
        if group_id == 0:
            state[step, :, 0:2, 8:72, :] = self.xrecv[step, 0].astype(F32)
            state[step, :, 18:20, 8:72, :] = self.xrecv[step, 1].astype(F32)
        for tile in range(first, first + count):
            self.stage[0] = self.yrecv[step, 0, tile].astype(F32)
            self.stage[1] = self.yrecv[step, 1, tile].astype(F32)
            packed = self.zrecv[step, tile].astype(F32)
            for t in range(2):
                for i, x in enumerate(TILES[tile]):
                    slab = 4 * t + i
                    state[step, t, 2 + x, 6:8, :] = self.stage[0, 2 * slab:2 * slab + 2, :]
                    state[step, t, 2 + x, 72:74, :] = self.stage[1, 2 * slab:2 * slab + 2, :]
                    for b in range(4):
                        self.ends[t, x, 16 * b:16 * b + 16, :] = pltpu.roll(
                            packed, (254 - 32 * b - 4 * slab) % 128, 1
                        )


def transport(vel, out_ref, halo):
    state = halo.state
    lane = lax.broadcasted_iota(jnp.int32, (16, 128), 1)
    wrapped = {-1: lane == 127, -2: lane >= 126, 1: lane == 0, 2: lane < 2}

    def compute(step, group_id, last):
        first, count = GROUPS[group_id]

        def plane(n, carry):
            x = n + jnp.where(n >= 2, 12, 0) if group_id == 0 else TILES[first][0] + n
            for y in range(0, 64, 16):
                speeds = [vel[d, x, y:y + 16, :] * (-TIME_STEP) for d in range(3)]
                upward = [s < 0.0 for s in speeds]
                one = [1.5 * s for s in speeds]
                two = [0.5 * s for s in speeds]
                for t in range(2):
                    conc = state[step, t, 2 + x, 8 + y:24 + y, :]
                    edge = halo.ends[t, x, y:y + 16, :]

                    def shifted_x(k):
                        return state[step, t, 2 + x + k, 8 + y:24 + y, :]

                    def shifted_y(k):
                        return state[step, t, 2 + x, 8 + y + k:24 + y + k, :]

                    def shifted_z(k):
                        return pltpu.roll(jnp.where(wrapped[k], edge, conc), -k % 128, 1)

                    total = conc
                    laplace = None
                    for d, shifted in enumerate((shifted_x, shifted_y, shifted_z)):
                        low, low_two, high, high_two = shifted(-1), shifted(-2), shifted(1), shifted(2)
                        below, above = conc - low, high - conc
                        near = jnp.where(upward[d], below, above)
                        far = jnp.where(upward[d], low - low_two, high_two - high)
                        total = total + one[d] * near - two[d] * far
                        bend = above - below
                        laplace = bend if laplace is None else laplace + bend
                    total = total + (TIME_STEP * RATES[t]) * laplace
                    if last:
                        out_ref[t, x, y:y + 16, :] = total
                    else:
                        state[step + 1, t, 2 + x, 8 + y:24 + y, :] = total
            return carry

        lax.fori_loop(0, 4 * count, plane, 0)

    def advance(step, last):
        for group_id in range(3):
            halo.receive(step, group_id)
            compute(step, group_id, last)
            if not last:
                halo.send(step + 1, group_id)

    def run(step, carry):
        advance(step, False)
        return carry

    lax.fori_loop(0, STEPS - 1, run, 0)
    advance(STEPS - 1, True)

    def finish(step, carry):
        for group_id in range(3):
            for copy in halo.copies(step, group_id):
                copy.wait_send()
        return carry

    lax.fori_loop(0, STEPS, finish, 0)


def fused(body_force, solid_mask, tracers, inlet_mask):
    fz, iz = z_tables()
    fx, ix = x_tables()
    ty = y_table()
    any_spec = pl.BlockSpec(memory_space=pl.ANY)
    vmem = pl.BlockSpec(memory_space=pltpu.VMEM)
    slab = (3, 16, 2, 32, 128)
    dma = pltpu.SemaphoreType.DMA
    return pl.pallas_call(
        fused_kernel,
        out_shape=(
            jax.ShapeDtypeStruct((3, 16, 64, 128), F32),
            jax.ShapeDtypeStruct((2, 16, 64, 128), F32),
        ),
        in_specs=[any_spec] * 9,
        out_specs=(vmem, vmem),
        scratch_shapes=[
            pltpu.VMEM((3, 16, 32, 256), BF16),
            pltpu.VMEM((16, 32, 256), jnp.int32),
            pltpu.VMEM((256, 256), BF16),
            pltpu.VMEM((256, 256), BF16),
            pltpu.VMEM((512, 1024), BF16),
            pltpu.VMEM((512, 512), BF16),
            pltpu.VMEM((512, 512), BF16),
            pltpu.VMEM((16, 32, 256), F32),
            pltpu.VMEM((1024, 256), BF16),
            pltpu.VMEM((8, 32, 512), BF16),
            pltpu.VMEM((3, 256, 512), F32),
            pltpu.VMEM((3, 256, 512), BF16),
            pltpu.VMEM((16, 32, 256), BF16),
        ]
        + [pltpu.VMEM(slab, BF16)] * 8
        + [pltpu.VMEM((3, 16, 32, 128), BF16)] * 2
        + [
            pltpu.VMEM((2, 64, 128), jnp.int32),
            pltpu.VMEM((STEPS, 2, 20, 80, 128), F32),
            pltpu.VMEM((2, 16, 64, 128), F32),
            pltpu.VMEM((2, 16, 128), F32),
        ]
        + [pltpu.VMEM((STEPS, 2, 2, 2, 64, 128), BF16)] * 2
        + [pltpu.VMEM((STEPS, 2, 4, 16, 128), BF16)] * 2
        + [pltpu.VMEM((STEPS, 4, 16, 128), BF16)] * 2
        + [dma((9,)), dma((4, 3)), dma((4, 3)), dma((3,)), dma((3,))]
        + [dma((STEPS, 2)), dma((STEPS, 2)), dma((STEPS, 3, 3)), dma((STEPS, 3, 3))],
        compiler_params=pltpu.CompilerParams(
            collective_id=0, has_side_effects=True, vmem_limit_bytes=VMEM_LIMIT
        ),
        name="stokes_transport",
    )(
        body_force, solid_mask, tracers, inlet_mask,
        jnp.asarray(fz), jnp.asarray(iz), jnp.asarray(ty), jnp.asarray(fx), jnp.asarray(ix),
    )


def solution(mesh):
    in_specs = (
        P(None, "gx", ("gy", "gz"), None),
        P("gx", ("gy", "gz"), None),
        P(None, "gx", "gy", "gz"),
        P(None, "gy", "gz"),
    )
    out_specs = (P(None, "gx", "gy", "gz"), P(None, "gx", "gy", "gz"))
    return jax.shard_map(fused, mesh=mesh, in_specs=in_specs, out_specs=out_specs, check_vma=False)
```

```python
import math

import jax
import jax.numpy as jnp
import numpy as np
from jax import lax
from jax.experimental import pallas as pl
from jax.experimental.pallas import tpu as pltpu
from jax.sharding import PartitionSpec as P

STEPS = 4
VISCOSITY = 0.0625
SCREENING = 0.25
TIME_STEP = 0.1
RATES = (0.05, 0.15)

MESH = pl.DeviceIdType.MESH
BF16 = jnp.bfloat16
F32 = jnp.float32
GRID_X, GRID_Y, GRID_Z = 256, 512, 256
KZ = GRID_Z // 2
VMEM_LIMIT = 60 * 1024 * 1024


def cos_sin(length):
    index = np.arange(length)
    phase = (index[:, None] * index[None, :] % length) * (2.0 * math.pi / length)
    return np.cos(phase), np.sin(phase)


def z_tables():
    cos_t, sin_t = cos_sin(GRID_Z)
    forward = np.concatenate([cos_t[:, :KZ], -sin_t[:, :KZ]], axis=1)
    forward[:, KZ] = cos_t[:, KZ]
    inverse = np.concatenate([2.0 * cos_t[:KZ], -2.0 * sin_t[:KZ]], axis=0)
    inverse[0] = cos_t[0]
    inverse[KZ] = cos_t[KZ]
    return forward.astype(jnp.bfloat16), inverse.astype(jnp.bfloat16)


def y_table():
    cos_t, sin_t = cos_sin(GRID_Y)
    return np.concatenate([cos_t, sin_t], axis=1).astype(jnp.bfloat16)


def x_tables():
    cos_t, sin_t = cos_sin(GRID_X)
    order = np.arange(GRID_X).reshape(2, 8, 16).transpose(0, 2, 1).reshape(-1)
    cos_p, sin_p = cos_t[order], sin_t[order]
    forward = np.block([[cos_p, -sin_p], [sin_p, cos_p]])
    inverse = np.block([[cos_p.T, sin_p.T], [-sin_p.T, cos_p.T]])
    return forward.astype(jnp.bfloat16), inverse.astype(jnp.bfloat16)


def swap_index_and_lanes(parts, unit):
    lane = lax.broadcasted_iota(jnp.int32, parts[0].shape, 1)
    step = 1
    while step < len(parts):
        shift = unit * step
        upper = (lane & shift) != 0
        after = list(parts)
        for a in range(len(parts)):
            if a & step:
                continue
            low, high = parts[a], parts[a | step]
            after[a] = jnp.where(upper, pltpu.roll(high, shift, 1), low)
            after[a | step] = jnp.where(upper, high, pltpu.roll(low, 128 - shift, 1))
        parts = after
        step *= 2
    return parts


def signed_wave(index, length):
    signed = jnp.where(index < length // 2, index, index - length)
    signed = jnp.where(index == length // 2, 0, signed)
    return signed.astype(F32) * (2.0 * math.pi / length)


TILES = ((0, 1, 14, 15), (2, 3, 4, 5), (6, 7, 8, 9), (10, 11, 12, 13))
GROUPS = ((0, 1), (1, 1), (2, 2))


def fused_kernel(
    force_hbm, mask_hbm, tracers_hbm, inlet_hbm, fz_hbm, iz_hbm, ty_hbm, fx_hbm, ix_hbm, vel_ref, out_ref,
    force, mask, fz, iz, ty, fx, ix, zbuf, rhs, xin, spec, green, zin,
    send1, recv1, send2, recv2, send3, recv3, send4, recv4, sendv, recvv,
    inlet, state, ends, stage, xsend, xrecv, ysend, yrecv, zsend, zrecv,
    load_sem, send_sem, recv_sem, vsend_sem, vrecv_sem, xs_sem, xr_sem, fs_sem, fr_sem,
):
    gx, gy, gz = lax.axis_index("gx"), lax.axis_index("gy"), lax.axis_index("gz")
    group = gy * 2 + gz

    def in_plane(to):
        return (gx, to // 2, to % 2)

    def in_column(to):
        return (to, gy, gz)

    loads = [
        pltpu.make_async_copy(src, dst, load_sem.at[n])
        for n, (src, dst) in enumerate(
            [(fz_hbm, fz), (mask_hbm, mask), (force_hbm, force), (ty_hbm, ty), (fx_hbm, fx), (ix_hbm, ix), (iz_hbm, iz),
             (inlet_hbm, inlet), (tracers_hbm, state.at[0, :, pl.ds(2, 16), pl.ds(8, 64)])]
        )
    ]
    for load in loads:
        load.start()

    barrier = pltpu.get_barrier_semaphore()

    def greet(k, carry):
        pl.semaphore_signal(barrier, inc=1, device_id=in_plane((group + k) % 16), device_id_type=MESH)
        pl.semaphore_signal(barrier, inc=1, device_id=in_column((gx + k) % 16), device_id_type=MESH)
        return carry

    lax.fori_loop(1, 16, greet, 0)

    def exchange(row, c, n, send, recv, me, place):
        def one(k, carry):
            to = (me + k) % 16
            pltpu.make_async_remote_copy(
                src_ref=send.at[n, to], dst_ref=recv.at[n, me],
                send_sem=send_sem.at[row, c], recv_sem=recv_sem.at[row, c],
                device_id=place(to), device_id_type=MESH,
            ).start()
            return carry

        lax.fori_loop(1, 16, one, 0)
        pltpu.make_async_copy(send.at[n, me], recv.at[n, me], recv_sem.at[row, c]).start()

    def arrived(row, c, n, recv):
        pltpu.make_async_copy(recv.at[n], recv.at[n], recv_sem.at[row, c]).wait()

    def sent(row, c, n, send):
        pltpu.make_async_copy(send.at[n, pl.ds(0, 15)], send.at[n, pl.ds(0, 15)], send_sem.at[row, c]).wait()

    for load in loads[:3]:
        load.wait()

    def forward_z(c, carry):
        for h in range(2):
            rows = slice(8 * h, 8 * h + 8)
            kept = jnp.where(mask[rows] == 0, force[c, rows].astype(F32), 0.0).astype(BF16)
            out = jnp.dot(kept.reshape(256, 256), fz[...], preferred_element_type=F32)
            zin[rows] = out.astype(BF16).reshape(8, 32, 256)
        for ri in range(2):
            for y in (0, 16):
                parts = [zin[x, y:y + 16, 128 * ri:128 * ri + 128] for x in range(16)]
                parts = swap_index_and_lanes(parts, 8)
                for to in range(16):
                    send1[c, to, ri, y:y + 16, :] = parts[to]

        @pl.when(c == 0)
        def _():
            pl.semaphore_wait(barrier, 30)

        exchange(0, c, c, send1, recv1, group, in_plane)
        return carry

    lax.fori_loop(0, 3, forward_z, 0)

    loads[3].wait()

    def forward_y(c, carry):
        arrived(0, c, c, recv1)
        re = recv1[c, :, 0].reshape(16, 2, 16, 128)
        im = recv1[c, :, 1].reshape(16, 2, 16, 128)
        rhs[0, :, :, :, 0:128] = re
        rhs[0, :, :, :, 128:256] = im
        rhs[1, :, :, :, 0:128] = im
        rhs[1, :, :, :, 128:256] = -re
        for m in range(2):
            out = jnp.dot(
                ty[256 * m:256 * m + 256, :], rhs[...].reshape(1024, 256), preferred_element_type=F32
            )
            out = out.astype(BF16).reshape(8, 2, 16, 256)
            for h in range(2):
                for ro in range(2):
                    send2[3 * h + c, 8 * m:8 * m + 8, ro] = out[:, h, :, 128 * ro:128 * ro + 128]
        exchange(1, c, c, send2, recv2, gx, in_column)
        return carry

    lax.fori_loop(0, 3, forward_y, 0)

    def second_half(c, carry):
        exchange(2, c, 3 + c, send2, recv2, gx, in_column)
        return carry

    lax.fori_loop(0, 3, second_half, 0)

    halo = Halo(state, ends, stage, xsend, xrecv, ysend, yrecv, zsend, zrecv, xs_sem, xr_sem, fs_sem, fr_sem)
    loads[7].wait()
    loads[8].wait()
    for t in range(2):
        plane = state[0, t, 2, 8:72, :]
        state[0, t, 2, 8:72, :] = jnp.where(gx == 0, jnp.where(inlet[t] == 1, 1.0, plane), plane)
    for group_id in range(3):
        halo.send(0, group_id)

    loads[4].wait()
    loads[5].wait()
    wave_x = signed_wave(lax.broadcasted_iota(jnp.int32, (16, GRID_X), 1), GRID_X)
    row = lax.broadcasted_iota(jnp.int32, (16, GRID_X), 0)

    def middle(h, carry):
        def forward_x(c, carry):
            n = 3 * h + c
            arrived(1 + h, c, n, recv2)
            for ri in range(2):
                for hi in range(2):
                    parts = [recv2[n, 8 * hi + i, ri] for i in range(8)]
                    parts = swap_index_and_lanes(parts, 1)
                    first = 256 * ri + 128 * hi
                    for k in range(8):
                        xin[c, k, :, first:first + 128] = parts[k]
            return carry

        lax.fori_loop(0, 3, forward_x, 0)
        spec[...] = jnp.dot(xin[...].reshape(384, 512), fx[...], preferred_element_type=F32).reshape(3, 8, 16, 512)

        def project(k, carry):
            wave_y = signed_wave(gx * 32 + h * 16 + row, GRID_Y)
            wave_z = signed_wave(group * 8 + k + jnp.zeros_like(row), GRID_Z)
            wave_sq = wave_x * wave_x + wave_y * wave_y + wave_z * wave_z
            gain = 1.0 / ((VISCOSITY * wave_sq + SCREENING) * float(GRID_X * GRID_Y * GRID_Z))
            inverse_sq = jnp.where(wave_sq > 0, 1.0 / jnp.where(wave_sq > 0, wave_sq, 1.0), 0.0)
            waves = (wave_x, wave_y, wave_z)
            for lanes in (slice(0, 256), slice(256, 512)):
                parts = [spec[c, k, :, lanes] for c in range(3)]
                inner = waves[0] * parts[0] + waves[1] * parts[1] + waves[2] * parts[2]
                along = inner * inverse_sq
                for c in range(3):
                    green[c, k, :, lanes] = (gain * (parts[c] - waves[c] * along)).astype(BF16)
            return carry

        lax.fori_loop(0, 8, project, 0)
        back = jnp.dot(green[...].reshape(384, 512), ix[...], preferred_element_type=F32)
        xin[...] = back.astype(BF16).reshape(3, 8, 16, 512)

        def inverse_x(c, carry):
            n = 3 * h + c
            for ro in range(2):
                for hi in range(2):
                    first = 256 * ro + 128 * hi
                    parts = [xin[c, k, :, first:first + 128] for k in range(8)]
                    parts = swap_index_and_lanes(parts, 1)
                    for i in range(8):
                        send3[n, 8 * hi + i, ro] = parts[i]
            exchange(3 + h, c, n, send3, recv3, gx, in_column)
            return carry

        lax.fori_loop(0, 3, inverse_x, 0)
        return carry

    lax.fori_loop(0, 2, middle, 0)

    def inverse_y(c, carry):
        for h in range(2):
            n = 3 * h + c
            arrived(3 + h, c, n, recv3)
            re, im = recv3[n, :, 0], recv3[n, :, 1]
            rhs[0, :, h, :, 0:128] = re
            rhs[0, :, h, :, 128:256] = im
            rhs[1, :, h, :, 0:128] = -im
            rhs[1, :, h, :, 128:256] = re
        for m in range(2):
            out = jnp.dot(
                ty[256 * m:256 * m + 256, :], rhs[...].reshape(1024, 256), preferred_element_type=F32
            )
            out = out.astype(BF16).reshape(8, 32, 256)
            send4[c, 8 * m:8 * m + 8, 0] = out[:, :, 0:128]
            send4[c, 8 * m:8 * m + 8, 1] = out[:, :, 128:256]
        exchange(5, c, c, send4, recv4, group, in_plane)
        return carry

    lax.fori_loop(0, 3, inverse_y, 0)

    loads[6].wait()
    own = pl.multiple_of(gz * 32, 32)
    other = pl.multiple_of((1 - gz) * 32, 32)

    def to_partner(c):
        return pltpu.make_async_remote_copy(
            src_ref=sendv.at[c], dst_ref=recvv.at[c], send_sem=vsend_sem.at[c], recv_sem=vrecv_sem.at[c],
            device_id=(gx, gy, 1 - gz), device_id_type=MESH,
        )

    def inverse_z(c, carry):
        arrived(5, c, c, recv4)
        for ro in range(2):
            for y in (0, 16):
                parts = [recv4[c, s, ro, y:y + 16, :] for s in range(16)]
                parts = swap_index_and_lanes(parts, 8)
                for x in range(16):
                    zin[x, y:y + 16, 128 * ro:128 * ro + 128] = parts[x]
        for h in range(2):
            rows = slice(8 * h, 8 * h + 8)
            out = jnp.dot(zin[rows].reshape(256, 256), iz[...], preferred_element_type=F32)
            zbuf[rows] = out.reshape(8, 32, 256)
        mine = pl.ds(pl.multiple_of(gz * 128, 128), 128)
        theirs = pl.ds(pl.multiple_of((1 - gz) * 128, 128), 128)
        sendv[c] = zbuf[:, :, theirs].astype(BF16)
        to_partner(c).start()
        vel_ref[c, :, pl.ds(own, 32), :] = zbuf[:, :, mine]
        return carry

    lax.fori_loop(0, 3, inverse_z, 0)

    def gather(c, carry):
        to_partner(c).wait_recv()
        vel_ref[c, :, pl.ds(other, 32), :] = recvv[c].astype(F32)
        return carry

    lax.fori_loop(0, 3, gather, 0)

    transport(vel_ref, out_ref, halo)

    def finish(c, carry):
        sent(0, c, c, send1)
        for h in range(2):
            sent(1 + h, c, 3 * h + c, send2)
            sent(3 + h, c, 3 * h + c, send3)
        sent(5, c, c, send4)
        to_partner(c).wait_send()
        return carry

    lax.fori_loop(0, 3, finish, 0)


class Halo:
    def __init__(self, state, ends, stage, xsend, xrecv, ysend, yrecv, zsend, zrecv, xs_sem, xr_sem, fs_sem, fr_sem):
        self.state, self.ends, self.stage = state, ends, stage
        self.xsend, self.xrecv, self.ysend, self.yrecv = xsend, xrecv, ysend, yrecv
        self.zsend, self.zrecv = zsend, zrecv
        self.xs_sem, self.xr_sem, self.fs_sem, self.fr_sem = xs_sem, xr_sem, fs_sem, fr_sem

    def copies(self, step, group_id):
        gx, gy, gz = lax.axis_index("gx"), lax.axis_index("gy"), lax.axis_index("gz")

        def remote(src, dst, send, recv, place):
            return pltpu.make_async_remote_copy(
                src_ref=src, dst_ref=dst, send_sem=send, recv_sem=recv, device_id=place, device_id_type=MESH
            )

        tiles = pl.ds(*GROUPS[group_id])
        found = [
            remote(self.ysend.at[step, side, tiles], self.yrecv.at[step, side, tiles],
                   self.fs_sem.at[step, group_id, side], self.fr_sem.at[step, group_id, side], place)
            for side, place in enumerate(((gx, (gy + 1) % 8, gz), (gx, (gy + 7) % 8, gz)))
        ]
        found.append(
            remote(self.zsend.at[step, tiles], self.zrecv.at[step, tiles],
                   self.fs_sem.at[step, group_id, 2], self.fr_sem.at[step, group_id, 2], (gx, gy, 1 - gz))
        )
        if group_id == 0:
            found += [
                remote(self.xsend.at[step, side], self.xrecv.at[step, side],
                       self.xs_sem.at[step, side], self.xr_sem.at[step, side], place)
                for side, place in enumerate((((gx + 1) % 16, gy, gz), ((gx + 15) % 16, gy, gz)))
            ]
        return found

    def send(self, step, group_id):
        state = self.state
        first, count = GROUPS[group_id]
        copies = self.copies(step, group_id)
        if group_id == 0:
            self.xsend[step, 0] = state[step, :, 16:18, 8:72, :].astype(BF16)
            self.xsend[step, 1] = state[step, :, 2:4, 8:72, :].astype(BF16)
            copies[3].start()
            copies[4].start()
        slot = lax.broadcasted_iota(jnp.int32, (16, 128), 1) // 4
        for tile in range(first, first + count):
            edges = [None] * 32
            for t in range(2):
                for i, x in enumerate(TILES[tile]):
                    slab = 4 * t + i
                    self.stage[0, 2 * slab:2 * slab + 2, :] = state[step, t, 2 + x, 70:72, :]
                    self.stage[1, 2 * slab:2 * slab + 2, :] = state[step, t, 2 + x, 8:10, :]
                    for b in range(4):
                        edges[8 * b + slab] = pltpu.roll(
                            state[step, t, 2 + x, 8 + 16 * b:24 + 16 * b, :].astype(BF16),
                            (2 + 32 * b + 4 * slab) % 128, 1,
                        )
            self.ysend[step, 0, tile] = self.stage[0].astype(BF16)
            self.ysend[step, 1, tile] = self.stage[1].astype(BF16)
            bit = 1
            while len(edges) > 1:
                edges = [jnp.where((slot & bit) != 0, edges[n + 1], edges[n]) for n in range(0, len(edges), 2)]
                bit *= 2
            self.zsend[step, tile] = edges[0]
        for copy in copies[:3]:
            copy.start()

    def receive(self, step, group_id):
        state = self.state
        first, count = GROUPS[group_id]
        for copy in self.copies(step, group_id):
            copy.wait_recv()
        if group_id == 0:
            state[step, :, 0:2, 8:72, :] = self.xrecv[step, 0].astype(F32)
            state[step, :, 18:20, 8:72, :] = self.xrecv[step, 1].astype(F32)
        for tile in range(first, first + count):
            self.stage[0] = self.yrecv[step, 0, tile].astype(F32)
            self.stage[1] = self.yrecv[step, 1, tile].astype(F32)
            packed = self.zrecv[step, tile]
            for t in range(2):
                for i, x in enumerate(TILES[tile]):
                    slab = 4 * t + i
                    state[step, t, 2 + x, 6:8, :] = self.stage[0, 2 * slab:2 * slab + 2, :]
                    state[step, t, 2 + x, 72:74, :] = self.stage[1, 2 * slab:2 * slab + 2, :]
                    for b in range(4):
                        self.ends[t, x, 16 * b:16 * b + 16, :] = pltpu.roll(
                            packed, (254 - 32 * b - 4 * slab) % 128, 1
                        ).astype(F32)


def transport(vel, out_ref, halo):
    state = halo.state
    lane = lax.broadcasted_iota(jnp.int32, (16, 128), 1)
    wrapped = {-1: lane == 127, -2: lane >= 126, 1: lane == 0, 2: lane < 2}

    def compute(step, group_id, last):
        first, count = GROUPS[group_id]

        def plane(n, carry):
            x = n + jnp.where(n >= 2, 12, 0) if group_id == 0 else TILES[first][0] + n
            for y in range(0, 64, 16):
                speeds = [vel[d, x, y:y + 16, :] * (-TIME_STEP) for d in range(3)]
                upward = [s < 0.0 for s in speeds]
                one = [1.5 * s for s in speeds]
                two = [0.5 * s for s in speeds]
                for t in range(2):
                    conc = state[step, t, 2 + x, 8 + y:24 + y, :]
                    edge = halo.ends[t, x, y:y + 16, :]

                    def shifted_x(k):
                        return state[step, t, 2 + x + k, 8 + y:24 + y, :]

                    def shifted_y(k):
                        return state[step, t, 2 + x, 8 + y + k:24 + y + k, :]

                    def shifted_z(k):
                        return pltpu.roll(jnp.where(wrapped[k], edge, conc), -k % 128, 1)

                    total = conc
                    laplace = None
                    for d, shifted in enumerate((shifted_x, shifted_y, shifted_z)):
                        low, low_two, high, high_two = shifted(-1), shifted(-2), shifted(1), shifted(2)
                        below, above = conc - low, high - conc
                        near = jnp.where(upward[d], below, above)
                        far = jnp.where(upward[d], low - low_two, high_two - high)
                        total = total + one[d] * near - two[d] * far
                        bend = above - below
                        laplace = bend if laplace is None else laplace + bend
                    total = total + (TIME_STEP * RATES[t]) * laplace
                    if last:
                        out_ref[t, x, y:y + 16, :] = total
                    else:
                        state[step + 1, t, 2 + x, 8 + y:24 + y, :] = total
            return carry

        lax.fori_loop(0, 4 * count, plane, 0)

    def advance(step, last):
        for group_id in range(3):
            halo.receive(step, group_id)
            compute(step, group_id, last)
            if not last:
                halo.send(step + 1, group_id)

    def run(step, carry):
        advance(step, False)
        return carry

    lax.fori_loop(0, STEPS - 1, run, 0)
    advance(STEPS - 1, True)

    def finish(step, carry):
        for group_id in range(3):
            for copy in halo.copies(step, group_id):
                copy.wait_send()
        return carry

    lax.fori_loop(0, STEPS, finish, 0)


def fused(body_force, solid_mask, tracers, inlet_mask):
    fz, iz = z_tables()
    fx, ix = x_tables()
    ty = y_table()
    any_spec = pl.BlockSpec(memory_space=pl.ANY)
    vmem = pl.BlockSpec(memory_space=pltpu.VMEM)
    slab = (3, 16, 2, 32, 128)
    half_slab = (6, 16, 2, 16, 128)
    dma = pltpu.SemaphoreType.DMA
    return pl.pallas_call(
        fused_kernel,
        out_shape=(
            jax.ShapeDtypeStruct((3, 16, 64, 128), F32),
            jax.ShapeDtypeStruct((2, 16, 64, 128), F32),
        ),
        in_specs=[any_spec] * 9,
        out_specs=(vmem, vmem),
        scratch_shapes=[
            pltpu.VMEM((3, 16, 32, 256), BF16),
            pltpu.VMEM((16, 32, 256), jnp.int32),
            pltpu.VMEM((256, 256), BF16),
            pltpu.VMEM((256, 256), BF16),
            pltpu.VMEM((512, 1024), BF16),
            pltpu.VMEM((512, 512), BF16),
            pltpu.VMEM((512, 512), BF16),
            pltpu.VMEM((16, 32, 256), F32),
            pltpu.VMEM((2, 16, 2, 16, 256), BF16),
            pltpu.VMEM((3, 8, 16, 512), BF16),
            pltpu.VMEM((3, 8, 16, 512), F32),
            pltpu.VMEM((3, 8, 16, 512), BF16),
            pltpu.VMEM((16, 32, 256), BF16),
        ]
        + [pltpu.VMEM(slab, BF16)] * 2
        + [pltpu.VMEM(half_slab, BF16)] * 4
        + [pltpu.VMEM(slab, BF16)] * 2
        + [pltpu.VMEM((3, 16, 32, 128), BF16)] * 2
        + [
            pltpu.VMEM((2, 64, 128), jnp.int32),
            pltpu.VMEM((STEPS, 2, 20, 80, 128), F32),
            pltpu.VMEM((2, 16, 64, 128), F32),
            pltpu.VMEM((2, 16, 128), F32),
        ]
        + [pltpu.VMEM((STEPS, 2, 2, 2, 64, 128), BF16)] * 2
        + [pltpu.VMEM((STEPS, 2, 4, 16, 128), BF16)] * 2
        + [pltpu.VMEM((STEPS, 4, 16, 128), BF16)] * 2
        + [dma((9,)), dma((6, 3)), dma((6, 3)), dma((3,)), dma((3,))]
        + [dma((STEPS, 2)), dma((STEPS, 2)), dma((STEPS, 3, 3)), dma((STEPS, 3, 3))],
        compiler_params=pltpu.CompilerParams(
            collective_id=0, has_side_effects=True, vmem_limit_bytes=VMEM_LIMIT
        ),
        name="stokes_transport",
    )(
        body_force, solid_mask, tracers, inlet_mask,
        jnp.asarray(fz), jnp.asarray(iz), jnp.asarray(ty), jnp.asarray(fx), jnp.asarray(ix),
    )


def solution(mesh):
    in_specs = (
        P(None, "gx", ("gy", "gz"), None),
        P("gx", ("gy", "gz"), None),
        P(None, "gx", "gy", "gz"),
        P(None, "gy", "gz"),
    )
    out_specs = (P(None, "gx", "gy", "gz"), P(None, "gx", "gy", "gz"))
    return jax.shard_map(fused, mesh=mesh, in_specs=in_specs, out_specs=out_specs, check_vma=False)
```

```python
import math

import jax
import jax.numpy as jnp
import numpy as np
from jax import lax
from jax.experimental import pallas as pl
from jax.experimental.pallas import tpu as pltpu
from jax.sharding import PartitionSpec as P

STEPS = 4
VISCOSITY = 0.0625
SCREENING = 0.25
TIME_STEP = 0.1
RATES = (0.05, 0.15)

MESH = pl.DeviceIdType.MESH
BF16 = jnp.bfloat16
F32 = jnp.float32
GRID_X, GRID_Y, GRID_Z = 256, 512, 256
KZ = GRID_Z // 2
VMEM_LIMIT = 60 * 1024 * 1024


def cos_sin(length):
    index = np.arange(length)
    phase = (index[:, None] * index[None, :] % length) * (2.0 * math.pi / length)
    return np.cos(phase), np.sin(phase)


def z_tables():
    cos_t, sin_t = cos_sin(GRID_Z)
    forward = np.concatenate([cos_t[:, :KZ], -sin_t[:, :KZ]], axis=1)
    forward[:, KZ] = cos_t[:, KZ]
    inverse = np.concatenate([2.0 * cos_t[:KZ], -2.0 * sin_t[:KZ]], axis=0)
    inverse[0] = cos_t[0]
    inverse[KZ] = cos_t[KZ]
    return forward.astype(jnp.bfloat16), inverse.astype(jnp.bfloat16)


def y_table():
    cos_t, sin_t = cos_sin(GRID_Y)
    return np.concatenate([cos_t, sin_t], axis=1).astype(jnp.bfloat16)


def x_tables():
    cos_t, sin_t = cos_sin(GRID_X)
    order = np.arange(GRID_X).reshape(2, 8, 16).transpose(0, 2, 1).reshape(-1)
    cos_p, sin_p = cos_t[order], sin_t[order]
    forward = np.block([[cos_p, -sin_p], [sin_p, cos_p]])
    inverse = np.block([[cos_p.T, sin_p.T], [-sin_p.T, cos_p.T]])
    return forward.astype(jnp.bfloat16), inverse.astype(jnp.bfloat16)


def swap_index_and_lanes(parts, unit):
    lane = lax.broadcasted_iota(jnp.int32, parts[0].shape, 1)
    step = 1
    while step < len(parts):
        shift = unit * step
        upper = (lane & shift) != 0
        after = list(parts)
        for a in range(len(parts)):
            if a & step:
                continue
            low, high = parts[a], parts[a | step]
            after[a] = jnp.where(upper, pltpu.roll(high, shift, 1), low)
            after[a | step] = jnp.where(upper, high, pltpu.roll(low, 128 - shift, 1))
        parts = after
        step *= 2
    return parts


def signed_wave(index, length):
    signed = jnp.where(index < length // 2, index, index - length)
    signed = jnp.where(index == length // 2, 0, signed)
    return signed.astype(F32) * (2.0 * math.pi / length)


TILES = ((0, 1, 14, 15), (2, 3, 4, 5), (6, 7, 8, 9), (10, 11, 12, 13))
GROUPS = ((0, 1), (1, 1), (2, 1), (3, 1))


def fused_kernel(
    force_hbm, mask_hbm, tracers_hbm, inlet_hbm, fz_hbm, iz_hbm, ty_hbm, fx_hbm, ix_hbm, vel_ref, out_ref,
    force, mask, fz, iz, ty, fx, ix, zbuf, rhs, xin, spec, green, zin,
    send1, recv1, send2, recv2, send3, recv3, send4, recv4, sendv, recvv,
    inlet, state, ends, stage, xsend, xrecv, ysend, yrecv, zsend, zrecv,
    load_sem, send_sem, recv_sem, vsend_sem, vrecv_sem, xs_sem, xr_sem, fs_sem, fr_sem,
):
    gx, gy, gz = lax.axis_index("gx"), lax.axis_index("gy"), lax.axis_index("gz")
    group = gy * 2 + gz

    def in_plane(to):
        return (gx, to // 2, to % 2)

    def in_column(to):
        return (to, gy, gz)

    loads = [
        pltpu.make_async_copy(src, dst, load_sem.at[n])
        for n, (src, dst) in enumerate(
            [(fz_hbm, fz), (mask_hbm, mask), (force_hbm, force), (ty_hbm, ty), (fx_hbm, fx), (ix_hbm, ix), (iz_hbm, iz),
             (inlet_hbm, inlet), (tracers_hbm, state.at[0, :, pl.ds(2, 16), pl.ds(8, 64)])]
        )
    ]
    for load in loads:
        load.start()

    barrier = pltpu.get_barrier_semaphore()

    def greet(k, carry):
        pl.semaphore_signal(barrier, inc=1, device_id=in_plane((group + k) % 16), device_id_type=MESH)
        pl.semaphore_signal(barrier, inc=1, device_id=in_column((gx + k) % 16), device_id_type=MESH)
        return carry

    lax.fori_loop(1, 16, greet, 0)

    def exchange(row, c, n, send, recv, me, place):
        def one(k, carry):
            to = (me + k) % 16
            pltpu.make_async_remote_copy(
                src_ref=send.at[n, to], dst_ref=recv.at[n, me],
                send_sem=send_sem.at[row, c], recv_sem=recv_sem.at[row, c],
                device_id=place(to), device_id_type=MESH,
            ).start()
            return carry

        for k in range(1, 16):
            one(k, 0)
        pltpu.make_async_copy(send.at[n, me], recv.at[n, me], recv_sem.at[row, c]).start()

    def arrived(row, c, n, recv):
        pltpu.make_async_copy(recv.at[n], recv.at[n], recv_sem.at[row, c]).wait()

    def sent(row, c, n, send):
        pltpu.make_async_copy(send.at[n, pl.ds(0, 15)], send.at[n, pl.ds(0, 15)], send_sem.at[row, c]).wait()

    for load in loads[:3]:
        load.wait()

    def forward_z(c, carry):
        for h in range(2):
            rows = slice(8 * h, 8 * h + 8)
            kept = jnp.where(mask[rows] == 0, force[c, rows].astype(F32), 0.0).astype(BF16)
            out = jnp.dot(kept.reshape(256, 256), fz[...], preferred_element_type=F32)
            zin[rows] = out.astype(BF16).reshape(8, 32, 256)
        for ri in range(2):
            for y in (0, 16):
                parts = [zin[x, y:y + 16, 128 * ri:128 * ri + 128] for x in range(16)]
                parts = swap_index_and_lanes(parts, 8)
                for to in range(16):
                    send1[c, to, ri, y:y + 16, :] = parts[to]

        @pl.when(c == 0)
        def _():
            pl.semaphore_wait(barrier, 30)

        exchange(0, c, c, send1, recv1, group, in_plane)
        return carry

    lax.fori_loop(0, 3, forward_z, 0)

    loads[3].wait()

    def forward_y(c, carry):
        arrived(0, c, c, recv1)
        re = recv1[c, :, 0].reshape(16, 2, 16, 128)
        im = recv1[c, :, 1].reshape(16, 2, 16, 128)
        rhs[0, :, :, :, 0:128] = re
        rhs[0, :, :, :, 128:256] = im
        rhs[1, :, :, :, 0:128] = im
        rhs[1, :, :, :, 128:256] = -re
        for m in range(2):
            out = jnp.dot(
                ty[256 * m:256 * m + 256, :], rhs[...].reshape(1024, 256), preferred_element_type=F32
            )
            out = out.astype(BF16).reshape(8, 2, 16, 256)
            for h in range(2):
                for ro in range(2):
                    send2[3 * h + c, 8 * m:8 * m + 8, ro] = out[:, h, :, 128 * ro:128 * ro + 128]
        exchange(1, c, c, send2, recv2, gx, in_column)
        return carry

    lax.fori_loop(0, 3, forward_y, 0)

    def second_half(c, carry):
        exchange(2, c, 3 + c, send2, recv2, gx, in_column)
        return carry

    lax.fori_loop(0, 3, second_half, 0)

    halo = Halo(state, ends, stage, xsend, xrecv, ysend, yrecv, zsend, zrecv, xs_sem, xr_sem, fs_sem, fr_sem)
    loads[7].wait()
    loads[8].wait()
    for t in range(2):
        plane = state[0, t, 2, 8:72, :]
        state[0, t, 2, 8:72, :] = jnp.where(gx == 0, jnp.where(inlet[t] == 1, 1.0, plane), plane)
    for group_id in range(len(GROUPS)):
        halo.send(0, group_id)

    loads[4].wait()
    loads[5].wait()
    wave_x = signed_wave(lax.broadcasted_iota(jnp.int32, (16, GRID_X), 1), GRID_X)
    row = lax.broadcasted_iota(jnp.int32, (16, GRID_X), 0)

    def middle(h, carry):
        def forward_x(c, carry):
            n = 3 * h + c
            arrived(1 + h, c, n, recv2)
            for ri in range(2):
                for hi in range(2):
                    parts = [recv2[n, 8 * hi + i, ri] for i in range(8)]
                    parts = swap_index_and_lanes(parts, 1)
                    first = 256 * ri + 128 * hi
                    for k in range(8):
                        xin[c, k, :, first:first + 128] = parts[k]
            return carry

        lax.fori_loop(0, 3, forward_x, 0)
        spec[...] = jnp.dot(xin[...].reshape(384, 512), fx[...], preferred_element_type=F32).reshape(3, 8, 16, 512)

        def project(k, carry):
            wave_y = signed_wave(gx * 32 + h * 16 + row, GRID_Y)
            wave_z = signed_wave(group * 8 + k + jnp.zeros_like(row), GRID_Z)
            wave_sq = wave_x * wave_x + wave_y * wave_y + wave_z * wave_z
            gain = 1.0 / ((VISCOSITY * wave_sq + SCREENING) * float(GRID_X * GRID_Y * GRID_Z))
            inverse_sq = jnp.where(wave_sq > 0, 1.0 / jnp.where(wave_sq > 0, wave_sq, 1.0), 0.0)
            waves = (wave_x, wave_y, wave_z)
            for lanes in (slice(0, 256), slice(256, 512)):
                parts = [spec[c, k, :, lanes] for c in range(3)]
                inner = waves[0] * parts[0] + waves[1] * parts[1] + waves[2] * parts[2]
                along = inner * inverse_sq
                for c in range(3):
                    green[c, k, :, lanes] = (gain * (parts[c] - waves[c] * along)).astype(BF16)
            return carry

        lax.fori_loop(0, 8, project, 0)
        back = jnp.dot(green[...].reshape(384, 512), ix[...], preferred_element_type=F32)
        xin[...] = back.astype(BF16).reshape(3, 8, 16, 512)

        def inverse_x(c, carry):
            n = 3 * h + c
            for ro in range(2):
                for hi in range(2):
                    first = 256 * ro + 128 * hi
                    parts = [xin[c, k, :, first:first + 128] for k in range(8)]
                    parts = swap_index_and_lanes(parts, 1)
                    for i in range(8):
                        send3[n, 8 * hi + i, ro] = parts[i]
            exchange(3 + h, c, n, send3, recv3, gx, in_column)
            return carry

        lax.fori_loop(0, 3, inverse_x, 0)
        return carry

    lax.fori_loop(0, 2, middle, 0)

    def inverse_y(c, carry):
        for h in range(2):
            n = 3 * h + c
            arrived(3 + h, c, n, recv3)
            re, im = recv3[n, :, 0], recv3[n, :, 1]
            rhs[0, :, h, :, 0:128] = re
            rhs[0, :, h, :, 128:256] = im
            rhs[1, :, h, :, 0:128] = -im
            rhs[1, :, h, :, 128:256] = re
        for m in range(2):
            out = jnp.dot(
                ty[256 * m:256 * m + 256, :], rhs[...].reshape(1024, 256), preferred_element_type=F32
            )
            out = out.astype(BF16).reshape(8, 32, 256)
            send4[c, 8 * m:8 * m + 8, 0] = out[:, :, 0:128]
            send4[c, 8 * m:8 * m + 8, 1] = out[:, :, 128:256]
        exchange(5, c, c, send4, recv4, group, in_plane)
        return carry

    lax.fori_loop(0, 3, inverse_y, 0)

    loads[6].wait()
    own = pl.multiple_of(gz * 32, 32)
    other = pl.multiple_of((1 - gz) * 32, 32)

    def to_partner(c):
        return pltpu.make_async_remote_copy(
            src_ref=sendv.at[c], dst_ref=recvv.at[c], send_sem=vsend_sem.at[c], recv_sem=vrecv_sem.at[c],
            device_id=(gx, gy, 1 - gz), device_id_type=MESH,
        )

    def inverse_z(c, carry):
        arrived(5, c, c, recv4)
        for ro in range(2):
            for y in (0, 16):
                parts = [recv4[c, s, ro, y:y + 16, :] for s in range(16)]
                parts = swap_index_and_lanes(parts, 8)
                for x in range(16):
                    zin[x, y:y + 16, 128 * ro:128 * ro + 128] = parts[x]
        for h in range(2):
            rows = slice(8 * h, 8 * h + 8)
            out = jnp.dot(zin[rows].reshape(256, 256), iz[...], preferred_element_type=F32)
            zbuf[rows] = out.reshape(8, 32, 256)
        mine = pl.ds(pl.multiple_of(gz * 128, 128), 128)
        theirs = pl.ds(pl.multiple_of((1 - gz) * 128, 128), 128)
        sendv[c] = zbuf[:, :, theirs].astype(BF16)
        to_partner(c).start()
        vel_ref[c, :, pl.ds(own, 32), :] = zbuf[:, :, mine]
        return carry

    lax.fori_loop(0, 3, inverse_z, 0)

    def gather(c, carry):
        to_partner(c).wait_recv()
        vel_ref[c, :, pl.ds(other, 32), :] = recvv[c].astype(F32)
        return carry

    lax.fori_loop(0, 3, gather, 0)

    transport(vel_ref, out_ref, halo)

    def finish(c, carry):
        sent(0, c, c, send1)
        for h in range(2):
            sent(1 + h, c, 3 * h + c, send2)
            sent(3 + h, c, 3 * h + c, send3)
        sent(5, c, c, send4)
        to_partner(c).wait_send()
        return carry

    lax.fori_loop(0, 3, finish, 0)


class Halo:
    def __init__(self, state, ends, stage, xsend, xrecv, ysend, yrecv, zsend, zrecv, xs_sem, xr_sem, fs_sem, fr_sem):
        self.state, self.ends, self.stage = state, ends, stage
        self.xsend, self.xrecv, self.ysend, self.yrecv = xsend, xrecv, ysend, yrecv
        self.zsend, self.zrecv = zsend, zrecv
        self.xs_sem, self.xr_sem, self.fs_sem, self.fr_sem = xs_sem, xr_sem, fs_sem, fr_sem

    def copies(self, step, group_id):
        gx, gy, gz = lax.axis_index("gx"), lax.axis_index("gy"), lax.axis_index("gz")

        def remote(src, dst, send, recv, place):
            return pltpu.make_async_remote_copy(
                src_ref=src, dst_ref=dst, send_sem=send, recv_sem=recv, device_id=place, device_id_type=MESH
            )

        tiles = pl.ds(*GROUPS[group_id])
        found = [
            remote(self.ysend.at[step, side, tiles], self.yrecv.at[step, side, tiles],
                   self.fs_sem.at[step, group_id, side], self.fr_sem.at[step, group_id, side], place)
            for side, place in enumerate(((gx, (gy + 1) % 8, gz), (gx, (gy + 7) % 8, gz)))
        ]
        found.append(
            remote(self.zsend.at[step, tiles], self.zrecv.at[step, tiles],
                   self.fs_sem.at[step, group_id, 2], self.fr_sem.at[step, group_id, 2], (gx, gy, 1 - gz))
        )
        if group_id == 0:
            found += [
                remote(self.xsend.at[step, side], self.xrecv.at[step, side],
                       self.xs_sem.at[step, side], self.xr_sem.at[step, side], place)
                for side, place in enumerate((((gx + 1) % 16, gy, gz), ((gx + 15) % 16, gy, gz)))
            ]
        return found

    def send(self, step, group_id):
        state = self.state
        first, count = GROUPS[group_id]
        copies = self.copies(step, group_id)
        if group_id == 0:
            self.xsend[step, 0] = state[step, :, 16:18, 8:72, :].astype(BF16)
            self.xsend[step, 1] = state[step, :, 2:4, 8:72, :].astype(BF16)
            copies[3].start()
            copies[4].start()
        slot = lax.broadcasted_iota(jnp.int32, (16, 128), 1) // 4
        for tile in range(first, first + count):
            edges = [None] * 32
            for t in range(2):
                for i, x in enumerate(TILES[tile]):
                    slab = 4 * t + i
                    self.stage[0, 2 * slab:2 * slab + 2, :] = state[step, t, 2 + x, 70:72, :]
                    self.stage[1, 2 * slab:2 * slab + 2, :] = state[step, t, 2 + x, 8:10, :]
                    for b in range(4):
                        edges[8 * b + slab] = pltpu.roll(
                            state[step, t, 2 + x, 8 + 16 * b:24 + 16 * b, :].astype(BF16),
                            (2 + 32 * b + 4 * slab) % 128, 1,
                        )
            self.ysend[step, 0, tile] = self.stage[0].astype(BF16)
            self.ysend[step, 1, tile] = self.stage[1].astype(BF16)
            bit = 1
            while len(edges) > 1:
                edges = [jnp.where((slot & bit) != 0, edges[n + 1], edges[n]) for n in range(0, len(edges), 2)]
                bit *= 2
            self.zsend[step, tile] = edges[0]
        for copy in copies[:3]:
            copy.start()

    def receive(self, step, group_id):
        state = self.state
        first, count = GROUPS[group_id]
        for copy in self.copies(step, group_id):
            copy.wait_recv()
        if group_id == 0:
            state[step, :, 0:2, 8:72, :] = self.xrecv[step, 0].astype(F32)
            state[step, :, 18:20, 8:72, :] = self.xrecv[step, 1].astype(F32)
        for tile in range(first, first + count):
            self.stage[0] = self.yrecv[step, 0, tile].astype(F32)
            self.stage[1] = self.yrecv[step, 1, tile].astype(F32)
            packed = self.zrecv[step, tile]
            for t in range(2):
                for i, x in enumerate(TILES[tile]):
                    slab = 4 * t + i
                    state[step, t, 2 + x, 6:8, :] = self.stage[0, 2 * slab:2 * slab + 2, :]
                    state[step, t, 2 + x, 72:74, :] = self.stage[1, 2 * slab:2 * slab + 2, :]
                    for b in range(4):
                        self.ends[t, x, 16 * b:16 * b + 16, :] = pltpu.roll(
                            packed, (254 - 32 * b - 4 * slab) % 128, 1
                        ).astype(F32)


def transport(vel, out_ref, halo):
    state = halo.state
    lane = lax.broadcasted_iota(jnp.int32, (16, 128), 1)
    wrapped = {-1: lane == 127, -2: lane >= 126, 1: lane == 0, 2: lane < 2}

    def compute(step, group_id, last):
        first, count = GROUPS[group_id]

        def plane(n, carry):
            x = n + jnp.where(n >= 2, 12, 0) if group_id == 0 else TILES[first][0] + n
            for y in range(0, 64, 16):
                speeds = [vel[d, x, y:y + 16, :] * (-TIME_STEP) for d in range(3)]
                upward = [s < 0.0 for s in speeds]
                one = [1.5 * s for s in speeds]
                two = [0.5 * s for s in speeds]
                for t in range(2):
                    conc = state[step, t, 2 + x, 8 + y:24 + y, :]
                    edge = halo.ends[t, x, y:y + 16, :]

                    def shifted_x(k):
                        return state[step, t, 2 + x + k, 8 + y:24 + y, :]

                    def shifted_y(k):
                        return state[step, t, 2 + x, 8 + y + k:24 + y + k, :]

                    def shifted_z(k):
                        return pltpu.roll(jnp.where(wrapped[k], edge, conc), -k % 128, 1)

                    total = conc
                    laplace = None
                    for d, shifted in enumerate((shifted_x, shifted_y, shifted_z)):
                        low, low_two, high, high_two = shifted(-1), shifted(-2), shifted(1), shifted(2)
                        below, above = conc - low, high - conc
                        near = jnp.where(upward[d], below, above)
                        far = jnp.where(upward[d], low - low_two, high_two - high)
                        total = total + one[d] * near - two[d] * far
                        bend = above - below
                        laplace = bend if laplace is None else laplace + bend
                    total = total + (TIME_STEP * RATES[t]) * laplace
                    if last:
                        out_ref[t, x, y:y + 16, :] = total
                    else:
                        state[step + 1, t, 2 + x, 8 + y:24 + y, :] = total
            return carry

        lax.fori_loop(0, 4 * count, plane, 0)

    def advance(step, last):
        for group_id in range(len(GROUPS)):
            halo.receive(step, group_id)
            compute(step, group_id, last)
            if not last:
                halo.send(step + 1, group_id)

    def run(step, carry):
        advance(step, False)
        return carry

    lax.fori_loop(0, STEPS - 1, run, 0)
    advance(STEPS - 1, True)

    def finish(step, carry):
        for group_id in range(len(GROUPS)):
            for copy in halo.copies(step, group_id):
                copy.wait_send()
        return carry

    lax.fori_loop(0, STEPS, finish, 0)


def fused(body_force, solid_mask, tracers, inlet_mask):
    fz, iz = z_tables()
    fx, ix = x_tables()
    ty = y_table()
    any_spec = pl.BlockSpec(memory_space=pl.ANY)
    vmem = pl.BlockSpec(memory_space=pltpu.VMEM)
    slab = (3, 16, 2, 32, 128)
    half_slab = (6, 16, 2, 16, 128)
    dma = pltpu.SemaphoreType.DMA
    return pl.pallas_call(
        fused_kernel,
        out_shape=(
            pltpu.VMEM((3, 16, 64, 128), F32),
            pltpu.VMEM((2, 16, 64, 128), F32),
        ),
        in_specs=[any_spec] * 9,
        out_specs=(vmem, vmem),
        scratch_shapes=[
            pltpu.VMEM((3, 16, 32, 256), BF16),
            pltpu.VMEM((16, 32, 256), jnp.int32),
            pltpu.VMEM((256, 256), BF16),
            pltpu.VMEM((256, 256), BF16),
            pltpu.VMEM((512, 1024), BF16),
            pltpu.VMEM((512, 512), BF16),
            pltpu.VMEM((512, 512), BF16),
            pltpu.VMEM((16, 32, 256), F32),
            pltpu.VMEM((2, 16, 2, 16, 256), BF16),
            pltpu.VMEM((3, 8, 16, 512), BF16),
            pltpu.VMEM((3, 8, 16, 512), F32),
            pltpu.VMEM((3, 8, 16, 512), BF16),
            pltpu.VMEM((16, 32, 256), BF16),
        ]
        + [pltpu.VMEM(slab, BF16)] * 2
        + [pltpu.VMEM(half_slab, BF16)] * 4
        + [pltpu.VMEM(slab, BF16)] * 2
        + [pltpu.VMEM((3, 16, 32, 128), BF16)] * 2
        + [
            pltpu.VMEM((2, 64, 128), jnp.int32),
            pltpu.VMEM((STEPS, 2, 20, 80, 128), F32),
            pltpu.VMEM((2, 16, 64, 128), F32),
            pltpu.VMEM((2, 16, 128), F32),
        ]
        + [pltpu.VMEM((STEPS, 2, 2, 2, 64, 128), BF16)] * 2
        + [pltpu.VMEM((STEPS, 2, 4, 16, 128), BF16)] * 2
        + [pltpu.VMEM((STEPS, 4, 16, 128), BF16)] * 2
        + [dma((9,)), dma((6, 3)), dma((6, 3)), dma((3,)), dma((3,))]
        + [dma((STEPS, 2)), dma((STEPS, 2)), dma((STEPS, len(GROUPS), 3)), dma((STEPS, len(GROUPS), 3))],
        compiler_params=pltpu.CompilerParams(
            collective_id=0, has_side_effects=True, vmem_limit_bytes=VMEM_LIMIT
        ),
        name="stokes_transport",
    )(
        body_force, solid_mask, tracers, inlet_mask,
        jnp.asarray(fz), jnp.asarray(iz), jnp.asarray(ty), jnp.asarray(fx), jnp.asarray(ix),
    )


def solution(mesh):
    in_specs = (
        P(None, "gx", ("gy", "gz"), None),
        P("gx", ("gy", "gz"), None),
        P(None, "gx", "gy", "gz"),
        P(None, "gy", "gz"),
    )
    out_specs = (P(None, "gx", "gy", "gz"), P(None, "gx", "gy", "gz"))
    return jax.shard_map(fused, mesh=mesh, in_specs=in_specs, out_specs=out_specs, check_vma=False)
```

```python
import math

import jax
import jax.numpy as jnp
import numpy as np
from jax import lax
from jax.experimental import pallas as pl
from jax.experimental.pallas import tpu as pltpu
from jax.sharding import PartitionSpec as P

STEPS = 4
VISCOSITY = 0.0625
SCREENING = 0.25
TIME_STEP = 0.1
RATES = (0.05, 0.15)

MESH = pl.DeviceIdType.MESH
BF16 = jnp.bfloat16
F32 = jnp.float32
GRID_X, GRID_Y, GRID_Z = 256, 512, 256
KZ = GRID_Z // 2
VMEM_LIMIT = 60 * 1024 * 1024


def cos_sin(length):
    index = np.arange(length)
    phase = (index[:, None] * index[None, :] % length) * (2.0 * math.pi / length)
    return np.cos(phase), np.sin(phase)


def z_tables():
    cos_t, sin_t = cos_sin(GRID_Z)
    forward = np.concatenate([cos_t[:, :KZ], -sin_t[:, :KZ]], axis=1)
    forward[:, KZ] = cos_t[:, KZ]
    inverse = np.concatenate([2.0 * cos_t[:KZ], -2.0 * sin_t[:KZ]], axis=0)
    inverse[0] = cos_t[0]
    inverse[KZ] = cos_t[KZ]
    return forward.astype(jnp.bfloat16), inverse.astype(jnp.bfloat16)


def y_table():
    cos_t, sin_t = cos_sin(GRID_Y)
    return np.concatenate([cos_t, sin_t], axis=1).astype(jnp.bfloat16)


def x_tables():
    cos_t, sin_t = cos_sin(GRID_X)
    order = np.arange(GRID_X).reshape(2, 8, 16).transpose(0, 2, 1).reshape(-1)
    cos_p, sin_p = cos_t[order], sin_t[order]
    forward = np.block([[cos_p, -sin_p], [sin_p, cos_p]])
    inverse = np.block([[cos_p.T, sin_p.T], [-sin_p.T, cos_p.T]])
    return forward.astype(jnp.bfloat16), inverse.astype(jnp.bfloat16)


def swap_index_and_lanes(parts, unit):
    lane = lax.broadcasted_iota(jnp.int32, parts[0].shape, 1)
    step = 1
    while step < len(parts):
        shift = unit * step
        upper = (lane & shift) != 0
        after = list(parts)
        for a in range(len(parts)):
            if a & step:
                continue
            low, high = parts[a], parts[a | step]
            after[a] = jnp.where(upper, pltpu.roll(high, shift, 1), low)
            after[a | step] = jnp.where(upper, high, pltpu.roll(low, 128 - shift, 1))
        parts = after
        step *= 2
    return parts


def signed_wave(index, length):
    signed = jnp.where(index < length // 2, index, index - length)
    signed = jnp.where(index == length // 2, 0, signed)
    return signed.astype(F32) * (2.0 * math.pi / length)


TILES = ((0, 1, 14, 15), (2, 3, 4, 5), (6, 7, 8, 9), (10, 11, 12, 13))
GROUPS = ((0, 1), (1, 1), (2, 1), (3, 1))


def fused_kernel(
    force_hbm, mask_hbm, tracers_hbm, inlet_hbm, fz_hbm, iz_hbm, ty_hbm, fx_hbm, ix_hbm, vel_ref, out_ref,
    force, mask, fz, iz, ty, fx, ix, zbuf, rhs, xin, spec, green, zin,
    send1, recv1, send2, recv2, send3, recv3, send4, recv4, sendv, recvv,
    inlet, state, ends, stage, xsend, xrecv, ysend, yrecv, zsend, zrecv,
    load_sem, send_sem, recv_sem, vsend_sem, vrecv_sem, xs_sem, xr_sem, fs_sem, fr_sem,
):
    gx, gy, gz = lax.axis_index("gx"), lax.axis_index("gy"), lax.axis_index("gz")
    group = gy * 2 + gz

    def in_plane(to):
        return (gx, to // 2, to % 2)

    def in_column(to):
        return (to, gy, gz)

    barrier = pltpu.get_barrier_semaphore()

    def greet(k, carry):
        pl.semaphore_signal(barrier, inc=1, device_id=in_plane((group + k) % 16), device_id_type=MESH)
        pl.semaphore_signal(barrier, inc=1, device_id=in_column((gx + k) % 16), device_id_type=MESH)
        return carry

    lax.fori_loop(1, 16, greet, 0)

    loads = [
        pltpu.make_async_copy(src, dst, load_sem.at[n])
        for n, (src, dst) in enumerate(
            [(fz_hbm, fz), (mask_hbm, mask), (force_hbm, force), (ty_hbm, ty), (fx_hbm, fx), (ix_hbm, ix), (iz_hbm, iz),
             (inlet_hbm, inlet), (tracers_hbm, state.at[0, :, pl.ds(2, 16), pl.ds(8, 64)])]
        )
    ]
    for load in loads:
        load.start()

    def exchange(row, c, n, send, recv, me, place):
        def one(k, carry):
            to = (me + k) % 16
            pltpu.make_async_remote_copy(
                src_ref=send.at[n, to], dst_ref=recv.at[n, me],
                send_sem=send_sem.at[row, c], recv_sem=recv_sem.at[row, c],
                device_id=place(to), device_id_type=MESH,
            ).start()
            return carry

        for k in range(1, 16):
            one(k, 0)
        pltpu.make_async_copy(send.at[n, me], recv.at[n, me], recv_sem.at[row, c]).start()

    def arrived(row, c, n, recv):
        pltpu.make_async_copy(recv.at[n], recv.at[n], recv_sem.at[row, c]).wait()

    def sent(row, c, n, send):
        pltpu.make_async_copy(send.at[n, pl.ds(0, 15)], send.at[n, pl.ds(0, 15)], send_sem.at[row, c]).wait()

    for load in loads[:3]:
        load.wait()

    def forward_z(c, carry):
        for h in range(2):
            rows = slice(8 * h, 8 * h + 8)
            kept = jnp.where(mask[rows] == 0, force[c, rows].astype(F32), 0.0).astype(BF16)
            out = jnp.dot(kept.reshape(256, 256), fz[...], preferred_element_type=F32)
            zin[rows] = out.astype(BF16).reshape(8, 32, 256)
        for ri in range(2):
            for y in (0, 16):
                parts = [zin[x, y:y + 16, 128 * ri:128 * ri + 128] for x in range(16)]
                parts = swap_index_and_lanes(parts, 8)
                for to in range(16):
                    send1[c, to, ri, y:y + 16, :] = parts[to]

        @pl.when(c == 0)
        def _():
            pl.semaphore_wait(barrier, 30)

        exchange(0, c, c, send1, recv1, group, in_plane)
        return carry

    lax.fori_loop(0, 3, forward_z, 0)

    loads[3].wait()

    def forward_y(c, carry):
        arrived(0, c, c, recv1)
        re = recv1[c, :, 0].reshape(16, 2, 16, 128)
        im = recv1[c, :, 1].reshape(16, 2, 16, 128)
        rhs[0, :, :, :, 0:128] = re
        rhs[0, :, :, :, 128:256] = im
        rhs[1, :, :, :, 0:128] = im
        rhs[1, :, :, :, 128:256] = -re
        for m in range(2):
            out = jnp.dot(
                ty[256 * m:256 * m + 256, :], rhs[...].reshape(1024, 256), preferred_element_type=F32
            )
            out = out.astype(BF16).reshape(8, 2, 16, 256)
            for h in range(2):
                for ro in range(2):
                    send2[3 * h + c, 8 * m:8 * m + 8, ro] = out[:, h, :, 128 * ro:128 * ro + 128]
        exchange(1, c, c, send2, recv2, gx, in_column)
        return carry

    lax.fori_loop(0, 3, forward_y, 0)

    def second_half(c, carry):
        exchange(2, c, 3 + c, send2, recv2, gx, in_column)
        return carry

    lax.fori_loop(0, 3, second_half, 0)

    halo = Halo(state, ends, stage, xsend, xrecv, ysend, yrecv, zsend, zrecv, xs_sem, xr_sem, fs_sem, fr_sem)
    loads[7].wait()
    loads[8].wait()
    for t in range(2):
        plane = state[0, t, 2, 8:72, :]
        state[0, t, 2, 8:72, :] = jnp.where(gx == 0, jnp.where(inlet[t] == 1, 1.0, plane), plane)
    for group_id in range(len(GROUPS)):
        halo.send(0, group_id)

    loads[4].wait()
    loads[5].wait()
    wave_x = signed_wave(lax.broadcasted_iota(jnp.int32, (16, GRID_X), 1), GRID_X)
    row = lax.broadcasted_iota(jnp.int32, (16, GRID_X), 0)

    def middle(h, carry):
        def forward_x(c, carry):
            n = 3 * h + c
            arrived(1 + h, c, n, recv2)
            for ri in range(2):
                for hi in range(2):
                    parts = [recv2[n, 8 * hi + i, ri] for i in range(8)]
                    parts = swap_index_and_lanes(parts, 1)
                    first = 256 * ri + 128 * hi
                    for k in range(8):
                        xin[c, k, :, first:first + 128] = parts[k]
            return carry

        lax.fori_loop(0, 3, forward_x, 0)
        spec[...] = jnp.dot(xin[...].reshape(384, 512), fx[...], preferred_element_type=F32).reshape(3, 8, 16, 512)

        def project(k, carry):
            wave_y = signed_wave(gx * 32 + h * 16 + row, GRID_Y)
            wave_z = signed_wave(group * 8 + k + jnp.zeros_like(row), GRID_Z)
            wave_sq = wave_x * wave_x + wave_y * wave_y + wave_z * wave_z
            gain = 1.0 / ((VISCOSITY * wave_sq + SCREENING) * float(GRID_X * GRID_Y * GRID_Z))
            inverse_sq = jnp.where(wave_sq > 0, 1.0 / jnp.where(wave_sq > 0, wave_sq, 1.0), 0.0)
            waves = (wave_x, wave_y, wave_z)
            for lanes in (slice(0, 256), slice(256, 512)):
                parts = [spec[c, k, :, lanes] for c in range(3)]
                inner = waves[0] * parts[0] + waves[1] * parts[1] + waves[2] * parts[2]
                along = inner * inverse_sq
                for c in range(3):
                    green[c, k, :, lanes] = (gain * (parts[c] - waves[c] * along)).astype(BF16)
            return carry

        lax.fori_loop(0, 8, project, 0)
        back = jnp.dot(green[...].reshape(384, 512), ix[...], preferred_element_type=F32)
        xin[...] = back.astype(BF16).reshape(3, 8, 16, 512)

        def inverse_x(c, carry):
            n = 3 * h + c
            for ro in range(2):
                for hi in range(2):
                    first = 256 * ro + 128 * hi
                    parts = [xin[c, k, :, first:first + 128] for k in range(8)]
                    parts = swap_index_and_lanes(parts, 1)
                    for i in range(8):
                        send3[n, 8 * hi + i, ro] = parts[i]

            @pl.when((h == 1) & (c > 0))
            def _():
                exchange(3, c, c, send3, recv3, gx, in_column)

            @pl.when((h == 1) | (c == 0))
            def _():
                exchange(3 + h, c, n, send3, recv3, gx, in_column)

            return carry

        lax.fori_loop(0, 3, inverse_x, 0)
        return carry

    lax.fori_loop(0, 2, middle, 0)

    def inverse_y(c, carry):
        for h in range(2):
            n = 3 * h + c
            arrived(3 + h, c, n, recv3)
            re, im = recv3[n, :, 0], recv3[n, :, 1]
            rhs[0, :, h, :, 0:128] = re
            rhs[0, :, h, :, 128:256] = im
            rhs[1, :, h, :, 0:128] = -im
            rhs[1, :, h, :, 128:256] = re
        for m in range(2):
            out = jnp.dot(
                ty[256 * m:256 * m + 256, :], rhs[...].reshape(1024, 256), preferred_element_type=F32
            )
            out = out.astype(BF16).reshape(8, 32, 256)
            send4[c, 8 * m:8 * m + 8, 0] = out[:, :, 0:128]
            send4[c, 8 * m:8 * m + 8, 1] = out[:, :, 128:256]
        exchange(5, c, c, send4, recv4, group, in_plane)
        return carry

    lax.fori_loop(0, 3, inverse_y, 0)

    loads[6].wait()
    own = pl.multiple_of(gz * 32, 32)
    other = pl.multiple_of((1 - gz) * 32, 32)

    def to_partner(c):
        return pltpu.make_async_remote_copy(
            src_ref=sendv.at[c], dst_ref=recvv.at[c], send_sem=vsend_sem.at[c], recv_sem=vrecv_sem.at[c],
            device_id=(gx, gy, 1 - gz), device_id_type=MESH,
        )

    def inverse_z(c, carry):
        arrived(5, c, c, recv4)
        for ro in range(2):
            for y in (0, 16):
                parts = [recv4[c, s, ro, y:y + 16, :] for s in range(16)]
                parts = swap_index_and_lanes(parts, 8)
                for x in range(16):
                    zin[x, y:y + 16, 128 * ro:128 * ro + 128] = parts[x]
        for h in range(2):
            rows = slice(8 * h, 8 * h + 8)
            out = jnp.dot(zin[rows].reshape(256, 256), iz[...], preferred_element_type=F32)
            zbuf[rows] = out.reshape(8, 32, 256)
        mine = pl.ds(pl.multiple_of(gz * 128, 128), 128)
        theirs = pl.ds(pl.multiple_of((1 - gz) * 128, 128), 128)
        sendv[c] = zbuf[:, :, theirs].astype(BF16)
        to_partner(c).start()
        vel_ref[c, :, pl.ds(own, 32), :] = zbuf[:, :, mine]
        return carry

    lax.fori_loop(0, 3, inverse_z, 0)

    def gather(c, carry):
        to_partner(c).wait_recv()
        vel_ref[c, :, pl.ds(other, 32), :] = recvv[c].astype(F32)
        return carry

    lax.fori_loop(0, 3, gather, 0)

    transport(vel_ref, out_ref, halo)

    def finish(c, carry):
        sent(0, c, c, send1)
        for h in range(2):
            sent(1 + h, c, 3 * h + c, send2)
            sent(3 + h, c, 3 * h + c, send3)
        sent(5, c, c, send4)
        to_partner(c).wait_send()
        return carry

    lax.fori_loop(0, 3, finish, 0)


class Halo:
    def __init__(self, state, ends, stage, xsend, xrecv, ysend, yrecv, zsend, zrecv, xs_sem, xr_sem, fs_sem, fr_sem):
        self.state, self.ends, self.stage = state, ends, stage
        self.xsend, self.xrecv, self.ysend, self.yrecv = xsend, xrecv, ysend, yrecv
        self.zsend, self.zrecv = zsend, zrecv
        self.xs_sem, self.xr_sem, self.fs_sem, self.fr_sem = xs_sem, xr_sem, fs_sem, fr_sem

    def copies(self, step, group_id):
        gx, gy, gz = lax.axis_index("gx"), lax.axis_index("gy"), lax.axis_index("gz")

        def remote(src, dst, send, recv, place):
            return pltpu.make_async_remote_copy(
                src_ref=src, dst_ref=dst, send_sem=send, recv_sem=recv, device_id=place, device_id_type=MESH
            )

        tiles = pl.ds(*GROUPS[group_id])
        found = [
            remote(self.ysend.at[step, side, tiles], self.yrecv.at[step, side, tiles],
                   self.fs_sem.at[step, group_id, side], self.fr_sem.at[step, group_id, side], place)
            for side, place in enumerate(((gx, (gy + 1) % 8, gz), (gx, (gy + 7) % 8, gz)))
        ]
        found.append(
            remote(self.zsend.at[step, tiles], self.zrecv.at[step, tiles],
                   self.fs_sem.at[step, group_id, 2], self.fr_sem.at[step, group_id, 2], (gx, gy, 1 - gz))
        )
        if group_id == 0:
            found += [
                remote(self.xsend.at[step, side], self.xrecv.at[step, side],
                       self.xs_sem.at[step, side], self.xr_sem.at[step, side], place)
                for side, place in enumerate((((gx + 1) % 16, gy, gz), ((gx + 15) % 16, gy, gz)))
            ]
        return found

    def send(self, step, group_id):
        state = self.state
        first, count = GROUPS[group_id]
        copies = self.copies(step, group_id)
        for tile in range(first, first + count):
            for t in range(2):
                for i, x in enumerate(TILES[tile]):
                    slab = 4 * t + i
                    self.stage[0, 2 * slab:2 * slab + 2, :] = state[step, t, 2 + x, 70:72, :]
                    self.stage[1, 2 * slab:2 * slab + 2, :] = state[step, t, 2 + x, 8:10, :]
            self.ysend[step, 0, tile] = self.stage[0].astype(BF16)
            self.ysend[step, 1, tile] = self.stage[1].astype(BF16)
        copies[0].start()
        copies[1].start()
        if group_id == 0:
            self.xsend[step, 0] = state[step, :, 16:18, 8:72, :].astype(BF16)
            self.xsend[step, 1] = state[step, :, 2:4, 8:72, :].astype(BF16)
            copies[3].start()
            copies[4].start()
        slot = lax.broadcasted_iota(jnp.int32, (16, 128), 1) // 4
        for tile in range(first, first + count):
            edges = [None] * 32
            for t in range(2):
                for i, x in enumerate(TILES[tile]):
                    slab = 4 * t + i
                    for b in range(4):
                        edges[8 * b + slab] = pltpu.roll(
                            state[step, t, 2 + x, 8 + 16 * b:24 + 16 * b, :].astype(BF16),
                            (2 + 32 * b + 4 * slab) % 128, 1,
                        )
            bit = 1
            while len(edges) > 1:
                edges = [jnp.where((slot & bit) != 0, edges[n + 1], edges[n]) for n in range(0, len(edges), 2)]
                bit *= 2
            self.zsend[step, tile] = edges[0]
        copies[2].start()

    def receive(self, step, group_id):
        state = self.state
        first, count = GROUPS[group_id]
        for copy in self.copies(step, group_id):
            copy.wait_recv()
        if group_id == 0:
            state[step, :, 0:2, 8:72, :] = self.xrecv[step, 0].astype(F32)
            state[step, :, 18:20, 8:72, :] = self.xrecv[step, 1].astype(F32)
        for tile in range(first, first + count):
            self.stage[0] = self.yrecv[step, 0, tile].astype(F32)
            self.stage[1] = self.yrecv[step, 1, tile].astype(F32)
            packed = self.zrecv[step, tile]
            for t in range(2):
                for i, x in enumerate(TILES[tile]):
                    slab = 4 * t + i
                    state[step, t, 2 + x, 6:8, :] = self.stage[0, 2 * slab:2 * slab + 2, :]
                    state[step, t, 2 + x, 72:74, :] = self.stage[1, 2 * slab:2 * slab + 2, :]
                    for b in range(4):
                        self.ends[t, x, 16 * b:16 * b + 16, :] = pltpu.roll(
                            packed, (254 - 32 * b - 4 * slab) % 128, 1
                        ).astype(F32)


def transport(vel, out_ref, halo):
    state = halo.state
    lane = lax.broadcasted_iota(jnp.int32, (16, 128), 1)
    wrapped = {-1: lane == 127, -2: lane >= 126, 1: lane == 0, 2: lane < 2}

    def compute(step, group_id, last):
        first, count = GROUPS[group_id]

        def plane(n, carry):
            x = n + jnp.where(n >= 2, 12, 0) if group_id == 0 else TILES[first][0] + n
            for y in range(0, 64, 16):
                speeds = [vel[d, x, y:y + 16, :] * (-TIME_STEP) for d in range(3)]
                upward = [s < 0.0 for s in speeds]
                one = [1.5 * s for s in speeds]
                two = [0.5 * s for s in speeds]
                for t in range(2):
                    conc = state[step, t, 2 + x, 8 + y:24 + y, :]
                    edge = halo.ends[t, x, y:y + 16, :]

                    def shifted_x(k):
                        return state[step, t, 2 + x + k, 8 + y:24 + y, :]

                    def shifted_y(k):
                        return state[step, t, 2 + x, 8 + y + k:24 + y + k, :]

                    def shifted_z(k):
                        return pltpu.roll(jnp.where(wrapped[k], edge, conc), -k % 128, 1)

                    total = conc
                    laplace = None
                    for d, shifted in enumerate((shifted_x, shifted_y, shifted_z)):
                        low, low_two, high, high_two = shifted(-1), shifted(-2), shifted(1), shifted(2)
                        below, above = conc - low, high - conc
                        near = jnp.where(upward[d], below, above)
                        far = jnp.where(upward[d], low - low_two, high_two - high)
                        total = total + one[d] * near - two[d] * far
                        bend = above - below
                        laplace = bend if laplace is None else laplace + bend
                    total = total + (TIME_STEP * RATES[t]) * laplace
                    if last:
                        out_ref[t, x, y:y + 16, :] = total
                    else:
                        state[step + 1, t, 2 + x, 8 + y:24 + y, :] = total
            return carry

        lax.fori_loop(0, 4 * count, plane, 0)

    def advance(step, last):
        for group_id in range(len(GROUPS)):
            halo.receive(step, group_id)
            compute(step, group_id, last)
            if not last:
                halo.send(step + 1, group_id)

    def run(step, carry):
        advance(step, False)
        return carry

    lax.fori_loop(0, STEPS - 1, run, 0)
    advance(STEPS - 1, True)

    def finish(step, carry):
        for group_id in range(len(GROUPS)):
            for copy in halo.copies(step, group_id):
                copy.wait_send()
        return carry

    lax.fori_loop(0, STEPS, finish, 0)


def fused(body_force, solid_mask, tracers, inlet_mask):
    fz, iz = z_tables()
    fx, ix = x_tables()
    ty = y_table()
    any_spec = pl.BlockSpec(memory_space=pl.ANY)
    vmem = pl.BlockSpec(memory_space=pltpu.VMEM)
    slab = (3, 16, 2, 32, 128)
    half_slab = (6, 16, 2, 16, 128)
    dma = pltpu.SemaphoreType.DMA
    return pl.pallas_call(
        fused_kernel,
        out_shape=(
            pltpu.VMEM((3, 16, 64, 128), F32),
            pltpu.VMEM((2, 16, 64, 128), F32),
        ),
        in_specs=[any_spec] * 9,
        out_specs=(vmem, vmem),
        scratch_shapes=[
            pltpu.VMEM((3, 16, 32, 256), BF16),
            pltpu.VMEM((16, 32, 256), jnp.int32),
            pltpu.VMEM((256, 256), BF16),
            pltpu.VMEM((256, 256), BF16),
            pltpu.VMEM((512, 1024), BF16),
            pltpu.VMEM((512, 512), BF16),
            pltpu.VMEM((512, 512), BF16),
            pltpu.VMEM((16, 32, 256), F32),
            pltpu.VMEM((2, 16, 2, 16, 256), BF16),
            pltpu.VMEM((3, 8, 16, 512), BF16),
            pltpu.VMEM((3, 8, 16, 512), F32),
            pltpu.VMEM((3, 8, 16, 512), BF16),
            pltpu.VMEM((16, 32, 256), BF16),
        ]
        + [pltpu.VMEM(slab, BF16)] * 2
        + [pltpu.VMEM(half_slab, BF16)] * 4
        + [pltpu.VMEM(slab, BF16)] * 2
        + [pltpu.VMEM((3, 16, 32, 128), BF16)] * 2
        + [
            pltpu.VMEM((2, 64, 128), jnp.int32),
            pltpu.VMEM((STEPS, 2, 20, 80, 128), F32),
            pltpu.VMEM((2, 16, 64, 128), F32),
            pltpu.VMEM((2, 16, 128), F32),
        ]
        + [pltpu.VMEM((STEPS, 2, 2, 2, 64, 128), BF16)] * 2
        + [pltpu.VMEM((STEPS, 2, 4, 16, 128), BF16)] * 2
        + [pltpu.VMEM((STEPS, 4, 16, 128), BF16)] * 2
        + [dma((9,)), dma((6, 3)), dma((6, 3)), dma((3,)), dma((3,))]
        + [dma((STEPS, 2)), dma((STEPS, 2)), dma((STEPS, len(GROUPS), 3)), dma((STEPS, len(GROUPS), 3))],
        compiler_params=pltpu.CompilerParams(
            collective_id=0, has_side_effects=True, vmem_limit_bytes=VMEM_LIMIT
        ),
        name="stokes_transport",
    )(
        body_force, solid_mask, tracers, inlet_mask,
        jnp.asarray(fz), jnp.asarray(iz), jnp.asarray(ty), jnp.asarray(fx), jnp.asarray(ix),
    )


def solution(mesh):
    in_specs = (
        P(None, "gx", ("gy", "gz"), None),
        P("gx", ("gy", "gz"), None),
        P(None, "gx", "gy", "gz"),
        P(None, "gy", "gz"),
    )
    out_specs = (P(None, "gx", "gy", "gz"), P(None, "gx", "gy", "gz"))
    return jax.shard_map(fused, mesh=mesh, in_specs=in_specs, out_specs=out_specs, check_vma=False)
```

```python
import math

import jax
import jax.numpy as jnp
import numpy as np
from jax import lax
from jax.experimental import pallas as pl
from jax.experimental.pallas import tpu as pltpu
from jax.sharding import PartitionSpec as P

STEPS = 4
VISCOSITY = 0.0625
SCREENING = 0.25
TIME_STEP = 0.1
RATES = (0.05, 0.15)

MESH = pl.DeviceIdType.MESH
BF16 = jnp.bfloat16
F32 = jnp.float32
GRID_X, GRID_Y, GRID_Z = 256, 512, 256
KZ = GRID_Z // 2
VMEM_LIMIT = 60 * 1024 * 1024


def cos_sin(length):
    index = np.arange(length)
    phase = (index[:, None] * index[None, :] % length) * (2.0 * math.pi / length)
    return np.cos(phase), np.sin(phase)


def z_tables():
    cos_t, sin_t = cos_sin(GRID_Z)
    forward = np.concatenate([cos_t[:, :KZ], -sin_t[:, :KZ]], axis=1)
    forward[:, KZ] = cos_t[:, KZ]
    inverse = np.concatenate([2.0 * cos_t[:KZ], -2.0 * sin_t[:KZ]], axis=0)
    inverse[0] = cos_t[0]
    inverse[KZ] = cos_t[KZ]
    return forward.astype(jnp.bfloat16), inverse.astype(jnp.bfloat16)


def y_table():
    cos_t, sin_t = cos_sin(GRID_Y)
    return np.concatenate([cos_t, sin_t], axis=1).astype(jnp.bfloat16)


def x_tables():
    cos_t, sin_t = cos_sin(GRID_X)
    order = np.arange(GRID_X).reshape(2, 8, 16).transpose(0, 2, 1).reshape(-1)
    cos_p, sin_p = cos_t[order], sin_t[order]
    forward = np.block([[cos_p, -sin_p], [sin_p, cos_p]])
    inverse = np.block([[cos_p.T, sin_p.T], [-sin_p.T, cos_p.T]])
    return forward.astype(jnp.bfloat16), inverse.astype(jnp.bfloat16)


def swap_index_and_lanes(parts, unit):
    lane = lax.broadcasted_iota(jnp.int32, parts[0].shape, 1)
    step = 1
    while step < len(parts):
        shift = unit * step
        upper = (lane & shift) != 0
        after = list(parts)
        for a in range(len(parts)):
            if a & step:
                continue
            low, high = parts[a], parts[a | step]
            after[a] = jnp.where(upper, pltpu.roll(high, shift, 1), low)
            after[a | step] = jnp.where(upper, high, pltpu.roll(low, 128 - shift, 1))
        parts = after
        step *= 2
    return parts


def signed_wave(index, length):
    signed = jnp.where(index < length // 2, index, index - length)
    signed = jnp.where(index == length // 2, 0, signed)
    return signed.astype(F32) * (2.0 * math.pi / length)


TILES = ((0, 1, 14, 15), (2, 3, 4, 5), (6, 7, 8, 9), (10, 11, 12, 13))
GROUPS = ((0, 1), (1, 1), (2, 1), (3, 1))


def fused_kernel(
    force_hbm, mask_hbm, tracers_hbm, inlet_hbm, fz_hbm, iz_hbm, ty_hbm, fx_hbm, ix_hbm, vel_ref, out_ref,
    force, mask, fz, iz, ty, fx, ix, zbuf, rhs, xin, spec, green, zin,
    send1, recv1, send2, recv2, send3, recv3, send4, recv4, sendv, recvv,
    inlet, state, ends, stage, xsend, xrecv, ysend, yrecv, zsend, zrecv,
    load_sem, send_sem, recv_sem, vsend_sem, vrecv_sem, xs_sem, xr_sem, fs_sem, fr_sem,
):
    gx, gy, gz = lax.axis_index("gx"), lax.axis_index("gy"), lax.axis_index("gz")
    group = gy * 2 + gz

    def in_plane(to):
        return (gx, to // 2, to % 2)

    def in_column(to):
        return (to, gy, gz)

    barrier = pltpu.get_barrier_semaphore()

    def greet(k, carry):
        pl.semaphore_signal(barrier, inc=1, device_id=in_plane((group + k) % 16), device_id_type=MESH)
        pl.semaphore_signal(barrier, inc=1, device_id=in_column((gx + k) % 16), device_id_type=MESH)
        return carry

    lax.fori_loop(1, 16, greet, 0)

    loads = [
        pltpu.make_async_copy(src, dst, load_sem.at[n])
        for n, (src, dst) in enumerate(
            [(fz_hbm, fz), (mask_hbm, mask), (force_hbm, force), (ty_hbm, ty), (fx_hbm, fx), (ix_hbm, ix), (iz_hbm, iz),
             (inlet_hbm, inlet), (tracers_hbm, state.at[0, :, pl.ds(2, 16), pl.ds(8, 64)])]
        )
    ]
    for load in loads:
        load.start()

    def exchange(row, c, n, send, recv, me, place):
        def one(k, carry):
            to = (me + k) % 16
            pltpu.make_async_remote_copy(
                src_ref=send.at[n, to], dst_ref=recv.at[n, me],
                send_sem=send_sem.at[row, c], recv_sem=recv_sem.at[row, c],
                device_id=place(to), device_id_type=MESH,
            ).start()
            return carry

        for k in range(1, 16):
            one(k, 0)
        pltpu.make_async_copy(send.at[n, me], recv.at[n, me], recv_sem.at[row, c]).start()

    def arrived(row, c, n, recv):
        pltpu.make_async_copy(recv.at[n], recv.at[n], recv_sem.at[row, c]).wait()

    def sent(row, c, n, send):
        pltpu.make_async_copy(send.at[n, pl.ds(0, 15)], send.at[n, pl.ds(0, 15)], send_sem.at[row, c]).wait()

    for load in loads[:3]:
        load.wait()

    def forward_z(c, carry):
        for h in range(2):
            rows = slice(8 * h, 8 * h + 8)
            kept = jnp.where(mask[rows] == 0, force[c, rows].astype(F32), 0.0).astype(BF16)
            out = jnp.dot(kept.reshape(256, 256), fz[...], preferred_element_type=F32)
            zin[rows] = out.astype(BF16).reshape(8, 32, 256)
        for ri in range(2):
            for y in (0, 16):
                parts = [zin[x, y:y + 16, 128 * ri:128 * ri + 128] for x in range(16)]
                parts = swap_index_and_lanes(parts, 8)
                for to in range(16):
                    send1[c, to, ri, y:y + 16, :] = parts[to]

        @pl.when(c == 0)
        def _():
            pl.semaphore_wait(barrier, 30)

        exchange(0, c, c, send1, recv1, group, in_plane)
        return carry

    lax.fori_loop(0, 3, forward_z, 0)

    loads[3].wait()

    def forward_y(c, carry):
        arrived(0, c, c, recv1)
        re = recv1[c, :, 0].reshape(16, 2, 16, 128)
        im = recv1[c, :, 1].reshape(16, 2, 16, 128)
        rhs[0, :, :, :, 0:128] = re
        rhs[0, :, :, :, 128:256] = im
        rhs[1, :, :, :, 0:128] = im
        rhs[1, :, :, :, 128:256] = -re
        for m in range(2):
            out = jnp.dot(
                ty[256 * m:256 * m + 256, :], rhs[...].reshape(1024, 256), preferred_element_type=F32
            )
            out = out.astype(BF16).reshape(8, 2, 16, 256)
            for h in range(2):
                for ro in range(2):
                    send2[3 * h + c, 8 * m:8 * m + 8, ro] = out[:, h, :, 128 * ro:128 * ro + 128]
        exchange(1, c, c, send2, recv2, gx, in_column)
        return carry

    lax.fori_loop(0, 3, forward_y, 0)

    def second_half(c, carry):
        exchange(2, c, 3 + c, send2, recv2, gx, in_column)
        return carry

    lax.fori_loop(0, 3, second_half, 0)

    halo = Halo(state, ends, stage, xsend, xrecv, ysend, yrecv, zsend, zrecv, xs_sem, xr_sem, fs_sem, fr_sem)
    loads[7].wait()
    loads[8].wait()
    for t in range(2):
        plane = state[0, t, 2, 8:72, :]
        state[0, t, 2, 8:72, :] = jnp.where(gx == 0, jnp.where(inlet[t] == 1, 1.0, plane), plane)
    for group_id in range(len(GROUPS)):
        halo.send(0, group_id)

    loads[4].wait()
    loads[5].wait()
    wave_x = signed_wave(lax.broadcasted_iota(jnp.int32, (16, GRID_X), 1), GRID_X)
    row = lax.broadcasted_iota(jnp.int32, (16, GRID_X), 0)

    def middle(h, carry):
        def forward_x(c, carry):
            n = 3 * h + c
            arrived(1 + h, c, n, recv2)
            for ri in range(2):
                for hi in range(2):
                    parts = [recv2[n, 8 * hi + i, ri] for i in range(8)]
                    parts = swap_index_and_lanes(parts, 1)
                    first = 256 * ri + 128 * hi
                    for k in range(8):
                        xin[c, k, :, first:first + 128] = parts[k]
            return carry

        lax.fori_loop(0, 3, forward_x, 0)
        spec[...] = jnp.dot(xin[...].reshape(384, 512), fx[...], preferred_element_type=F32).reshape(3, 8, 16, 512)

        def project(k, carry):
            wave_y = signed_wave(gx * 32 + h * 16 + row, GRID_Y)
            wave_z = signed_wave(group * 8 + k + jnp.zeros_like(row), GRID_Z)
            wave_sq = wave_x * wave_x + wave_y * wave_y + wave_z * wave_z
            gain = 1.0 / ((VISCOSITY * wave_sq + SCREENING) * float(GRID_X * GRID_Y * GRID_Z))
            inverse_sq = jnp.where(wave_sq > 0, 1.0 / jnp.where(wave_sq > 0, wave_sq, 1.0), 0.0)
            waves = (wave_x, wave_y, wave_z)
            for lanes in (slice(0, 256), slice(256, 512)):
                parts = [spec[c, k, :, lanes] for c in range(3)]
                inner = waves[0] * parts[0] + waves[1] * parts[1] + waves[2] * parts[2]
                along = inner * inverse_sq
                for c in range(3):
                    green[c, k, :, lanes] = (gain * (parts[c] - waves[c] * along)).astype(BF16)
            return carry

        lax.fori_loop(0, 8, project, 0)
        back = jnp.dot(green[...].reshape(384, 512), ix[...], preferred_element_type=F32)
        xin[...] = back.astype(BF16).reshape(3, 8, 16, 512)

        def inverse_x(c, carry):
            n = 3 * h + c
            for ro in range(2):
                for hi in range(2):
                    first = 256 * ro + 128 * hi
                    parts = [xin[c, k, :, first:first + 128] for k in range(8)]
                    parts = swap_index_and_lanes(parts, 1)
                    for i in range(8):
                        send3[n, 8 * hi + i, ro] = parts[i]

            @pl.when((h == 1) & (c > 0))
            def _():
                exchange(3, c, c, send3, recv3, gx, in_column)

            @pl.when((h == 1) | (c == 0))
            def _():
                exchange(3 + h, c, n, send3, recv3, gx, in_column)

            return carry

        lax.fori_loop(0, 3, inverse_x, 0)
        return carry

    lax.fori_loop(0, 2, middle, 0)

    def inverse_y(c, carry):
        for h in range(2):
            n = 3 * h + c
            arrived(3 + h, c, n, recv3)
            re, im = recv3[n, :, 0], recv3[n, :, 1]
            rhs[0, :, h, :, 0:128] = re
            rhs[0, :, h, :, 128:256] = im
            rhs[1, :, h, :, 0:128] = -im
            rhs[1, :, h, :, 128:256] = re
        for m in range(2):
            out = jnp.dot(
                ty[256 * m:256 * m + 256, :], rhs[...].reshape(1024, 256), preferred_element_type=F32
            )
            out = out.astype(BF16).reshape(8, 32, 256)
            send4[c, 8 * m:8 * m + 8, 0] = out[:, :, 0:128]
            send4[c, 8 * m:8 * m + 8, 1] = out[:, :, 128:256]
        exchange(5, c, c, send4, recv4, group, in_plane)
        return carry

    lax.fori_loop(0, 3, inverse_y, 0)

    loads[6].wait()
    own = pl.multiple_of(gz * 32, 32)
    other = pl.multiple_of((1 - gz) * 32, 32)

    def to_partner(c, h):
        planes = pl.ds(8 * h, 8)
        return pltpu.make_async_remote_copy(
            src_ref=sendv.at[c, planes], dst_ref=recvv.at[c, planes],
            send_sem=vsend_sem.at[c, h], recv_sem=vrecv_sem.at[c, h],
            device_id=(gx, gy, 1 - gz), device_id_type=MESH,
        )

    def inverse_z(c, carry):
        arrived(5, c, c, recv4)
        for ro in range(2):
            for y in (0, 16):
                parts = [recv4[c, s, ro, y:y + 16, :] for s in range(16)]
                parts = swap_index_and_lanes(parts, 8)
                for x in range(16):
                    zin[x, y:y + 16, 128 * ro:128 * ro + 128] = parts[x]
        mine = pl.ds(pl.multiple_of(gz * 128, 128), 128)
        theirs = pl.ds(pl.multiple_of((1 - gz) * 128, 128), 128)
        for h in range(2):
            rows = slice(8 * h, 8 * h + 8)
            out = jnp.dot(zin[rows].reshape(256, 256), iz[...], preferred_element_type=F32)
            zbuf[rows] = out.reshape(8, 32, 256)
            sendv[c, rows] = zbuf[rows, :, theirs].astype(BF16)
            to_partner(c, h).start()
        vel_ref[c, :, pl.ds(own, 32), :] = zbuf[:, :, mine]
        return carry

    lax.fori_loop(0, 3, inverse_z, 0)

    def gather(c, carry):
        for h in range(2):
            to_partner(c, h).wait_recv()
            rows = slice(8 * h, 8 * h + 8)
            vel_ref[c, rows, pl.ds(other, 32), :] = recvv[c, rows].astype(F32)
        return carry

    lax.fori_loop(0, 3, gather, 0)

    transport(vel_ref, out_ref, halo)

    def finish(c, carry):
        sent(0, c, c, send1)
        for h in range(2):
            sent(1 + h, c, 3 * h + c, send2)
            sent(3 + h, c, 3 * h + c, send3)
        sent(5, c, c, send4)
        for h in range(2):
            to_partner(c, h).wait_send()
        return carry

    lax.fori_loop(0, 3, finish, 0)


class Halo:
    def __init__(self, state, ends, stage, xsend, xrecv, ysend, yrecv, zsend, zrecv, xs_sem, xr_sem, fs_sem, fr_sem):
        self.state, self.ends, self.stage = state, ends, stage
        self.xsend, self.xrecv, self.ysend, self.yrecv = xsend, xrecv, ysend, yrecv
        self.zsend, self.zrecv = zsend, zrecv
        self.xs_sem, self.xr_sem, self.fs_sem, self.fr_sem = xs_sem, xr_sem, fs_sem, fr_sem

    def copies(self, step, group_id):
        gx, gy, gz = lax.axis_index("gx"), lax.axis_index("gy"), lax.axis_index("gz")

        def remote(src, dst, send, recv, place):
            return pltpu.make_async_remote_copy(
                src_ref=src, dst_ref=dst, send_sem=send, recv_sem=recv, device_id=place, device_id_type=MESH
            )

        tiles = pl.ds(*GROUPS[group_id])
        found = [
            remote(self.ysend.at[step, side, tiles], self.yrecv.at[step, side, tiles],
                   self.fs_sem.at[step, group_id, side], self.fr_sem.at[step, group_id, side], place)
            for side, place in enumerate(((gx, (gy + 1) % 8, gz), (gx, (gy + 7) % 8, gz)))
        ]
        found.append(
            remote(self.zsend.at[step, tiles], self.zrecv.at[step, tiles],
                   self.fs_sem.at[step, group_id, 2], self.fr_sem.at[step, group_id, 2], (gx, gy, 1 - gz))
        )
        if group_id == 0:
            found += [
                remote(self.xsend.at[step, side], self.xrecv.at[step, side],
                       self.xs_sem.at[step, side], self.xr_sem.at[step, side], place)
                for side, place in enumerate((((gx + 1) % 16, gy, gz), ((gx + 15) % 16, gy, gz)))
            ]
        return found

    def send(self, step, group_id):
        state = self.state
        first, count = GROUPS[group_id]
        copies = self.copies(step, group_id)
        for tile in range(first, first + count):
            for t in range(2):
                for i, x in enumerate(TILES[tile]):
                    slab = 4 * t + i
                    self.stage[0, 2 * slab:2 * slab + 2, :] = state[step, t, 2 + x, 70:72, :]
                    self.stage[1, 2 * slab:2 * slab + 2, :] = state[step, t, 2 + x, 8:10, :]
            self.ysend[step, 0, tile] = self.stage[0].astype(BF16)
            self.ysend[step, 1, tile] = self.stage[1].astype(BF16)
        copies[0].start()
        copies[1].start()
        if group_id == 0:
            self.xsend[step, 0] = state[step, :, 16:18, 8:72, :].astype(BF16)
            self.xsend[step, 1] = state[step, :, 2:4, 8:72, :].astype(BF16)
            copies[3].start()
            copies[4].start()
        slot = lax.broadcasted_iota(jnp.int32, (16, 128), 1) // 4
        for tile in range(first, first + count):
            edges = [None] * 32
            for t in range(2):
                for i, x in enumerate(TILES[tile]):
                    slab = 4 * t + i
                    for b in range(4):
                        edges[8 * b + slab] = pltpu.roll(
                            state[step, t, 2 + x, 8 + 16 * b:24 + 16 * b, :].astype(BF16),
                            (2 + 32 * b + 4 * slab) % 128, 1,
                        )
            bit = 1
            while len(edges) > 1:
                edges = [jnp.where((slot & bit) != 0, edges[n + 1], edges[n]) for n in range(0, len(edges), 2)]
                bit *= 2
            self.zsend[step, tile] = edges[0]
        copies[2].start()

    def receive(self, step, group_id):
        state = self.state
        first, count = GROUPS[group_id]
        for copy in self.copies(step, group_id):
            copy.wait_recv()
        if group_id == 0:
            state[step, :, 0:2, 8:72, :] = self.xrecv[step, 0].astype(F32)
            state[step, :, 18:20, 8:72, :] = self.xrecv[step, 1].astype(F32)
        for tile in range(first, first + count):
            self.stage[0] = self.yrecv[step, 0, tile].astype(F32)
            self.stage[1] = self.yrecv[step, 1, tile].astype(F32)
            packed = self.zrecv[step, tile]
            for t in range(2):
                for i, x in enumerate(TILES[tile]):
                    slab = 4 * t + i
                    state[step, t, 2 + x, 6:8, :] = self.stage[0, 2 * slab:2 * slab + 2, :]
                    state[step, t, 2 + x, 72:74, :] = self.stage[1, 2 * slab:2 * slab + 2, :]
                    for b in range(4):
                        self.ends[t, x, 16 * b:16 * b + 16, :] = pltpu.roll(
                            packed, (254 - 32 * b - 4 * slab) % 128, 1
                        ).astype(F32)


def transport(vel, out_ref, halo):
    state = halo.state
    lane = lax.broadcasted_iota(jnp.int32, (16, 128), 1)
    wrapped = {-1: lane == 127, -2: lane >= 126, 1: lane == 0, 2: lane < 2}

    def compute(step, group_id, last):
        first, count = GROUPS[group_id]

        def plane(n, carry):
            x = n + jnp.where(n >= 2, 12, 0) if group_id == 0 else TILES[first][0] + n
            for y in range(0, 64, 16):
                speeds = [vel[d, x, y:y + 16, :] * (-TIME_STEP) for d in range(3)]
                upward = [s < 0.0 for s in speeds]
                one = [1.5 * s for s in speeds]
                two = [0.5 * s for s in speeds]
                for t in range(2):
                    conc = state[step, t, 2 + x, 8 + y:24 + y, :]
                    edge = halo.ends[t, x, y:y + 16, :]

                    def shifted_x(k):
                        return state[step, t, 2 + x + k, 8 + y:24 + y, :]

                    def shifted_y(k):
                        return state[step, t, 2 + x, 8 + y + k:24 + y + k, :]

                    def shifted_z(k):
                        return pltpu.roll(jnp.where(wrapped[k], edge, conc), -k % 128, 1)

                    total = conc
                    laplace = None
                    for d, shifted in enumerate((shifted_x, shifted_y, shifted_z)):
                        low, low_two, high, high_two = shifted(-1), shifted(-2), shifted(1), shifted(2)
                        below, above = conc - low, high - conc
                        near = jnp.where(upward[d], below, above)
                        far = jnp.where(upward[d], low - low_two, high_two - high)
                        total = total + one[d] * near - two[d] * far
                        bend = above - below
                        laplace = bend if laplace is None else laplace + bend
                    total = total + (TIME_STEP * RATES[t]) * laplace
                    if last:
                        out_ref[t, x, y:y + 16, :] = total
                    else:
                        state[step + 1, t, 2 + x, 8 + y:24 + y, :] = total
            return carry

        lax.fori_loop(0, 4 * count, plane, 0)

    def advance(step, last):
        for group_id in range(len(GROUPS)):
            halo.receive(step, group_id)
            compute(step, group_id, last)
            if not last:
                halo.send(step + 1, group_id)

    def run(step, carry):
        advance(step, False)
        return carry

    lax.fori_loop(0, STEPS - 1, run, 0)
    advance(STEPS - 1, True)

    def finish(step, carry):
        for group_id in range(len(GROUPS)):
            for copy in halo.copies(step, group_id):
                copy.wait_send()
        return carry

    lax.fori_loop(0, STEPS, finish, 0)


def fused(body_force, solid_mask, tracers, inlet_mask):
    fz, iz = z_tables()
    fx, ix = x_tables()
    ty = y_table()
    any_spec = pl.BlockSpec(memory_space=pl.ANY)
    vmem = pl.BlockSpec(memory_space=pltpu.VMEM)
    slab = (3, 16, 2, 32, 128)
    half_slab = (6, 16, 2, 16, 128)
    dma = pltpu.SemaphoreType.DMA
    return pl.pallas_call(
        fused_kernel,
        out_shape=(
            pltpu.VMEM((3, 16, 64, 128), F32),
            pltpu.VMEM((2, 16, 64, 128), F32),
        ),
        in_specs=[any_spec] * 9,
        out_specs=(vmem, vmem),
        scratch_shapes=[
            pltpu.VMEM((3, 16, 32, 256), BF16),
            pltpu.VMEM((16, 32, 256), jnp.int32),
            pltpu.VMEM((256, 256), BF16),
            pltpu.VMEM((256, 256), BF16),
            pltpu.VMEM((512, 1024), BF16),
            pltpu.VMEM((512, 512), BF16),
            pltpu.VMEM((512, 512), BF16),
            pltpu.VMEM((16, 32, 256), F32),
            pltpu.VMEM((2, 16, 2, 16, 256), BF16),
            pltpu.VMEM((3, 8, 16, 512), BF16),
            pltpu.VMEM((3, 8, 16, 512), F32),
            pltpu.VMEM((3, 8, 16, 512), BF16),
            pltpu.VMEM((16, 32, 256), BF16),
        ]
        + [pltpu.VMEM(slab, BF16)] * 2
        + [pltpu.VMEM(half_slab, BF16)] * 4
        + [pltpu.VMEM(slab, BF16)] * 2
        + [pltpu.VMEM((3, 16, 32, 128), BF16)] * 2
        + [
            pltpu.VMEM((2, 64, 128), jnp.int32),
            pltpu.VMEM((STEPS, 2, 20, 80, 128), F32),
            pltpu.VMEM((2, 16, 64, 128), F32),
            pltpu.VMEM((2, 16, 128), F32),
        ]
        + [pltpu.VMEM((STEPS, 2, 2, 2, 64, 128), BF16)] * 2
        + [pltpu.VMEM((STEPS, 2, 4, 16, 128), BF16)] * 2
        + [pltpu.VMEM((STEPS, 4, 16, 128), BF16)] * 2
        + [dma((9,)), dma((6, 3)), dma((6, 3)), dma((3, 2)), dma((3, 2))]
        + [dma((STEPS, 2)), dma((STEPS, 2)), dma((STEPS, len(GROUPS), 3)), dma((STEPS, len(GROUPS), 3))],
        compiler_params=pltpu.CompilerParams(
            collective_id=0, has_side_effects=True, vmem_limit_bytes=VMEM_LIMIT
        ),
        name="stokes_transport",
    )(
        body_force, solid_mask, tracers, inlet_mask,
        jnp.asarray(fz), jnp.asarray(iz), jnp.asarray(ty), jnp.asarray(fx), jnp.asarray(ix),
    )


def solution(mesh):
    in_specs = (
        P(None, "gx", ("gy", "gz"), None),
        P("gx", ("gy", "gz"), None),
        P(None, "gx", "gy", "gz"),
        P(None, "gy", "gz"),
    )
    out_specs = (P(None, "gx", "gy", "gz"), P(None, "gx", "gy", "gz"))
    return jax.shard_map(fused, mesh=mesh, in_specs=in_specs, out_specs=out_specs, check_vma=False)
```
